128 devices in a mesh: front: 4 (over x), row: 4 (over y), col: 8 (over z, core).
Axes of the slice: x: 4, y: 4, z: 4, core: 2. Of those that a mesh axis runs over, the one named last changes fastest.
Arguments:
- front_in: float32 [32768, 8192], P(('front', 'row'), 'col'), parts along dimension 0, may hold values from -6 to 6
- child_tiles: bfloat16 [128, 224, 128, 128], P(('front', 'row', 'col')), parts along dimension 0, may hold values from -6 to 6
- child_map: int32 [128, 224], P(('front', 'row', 'col')), parts along dimension 0, may hold values from 0 to 4095, as said below
- pattern: int32 [256, 64], P('front'), parts along dimension 0, may hold values 0 or 1
- pivot_inverse: float32 [8, 512, 512], P('front'), parts along dimension 0, may hold values from -0.01171875 to 0.01171875
Outputs:
- front_out: float32 [32768, 8192], P(('front', 'row'), 'col'), parts along dimension 0
The draws below stay inside these ranges and needn't reach their ends.
There are 4 independent parts, one for each index of `front`. The reference program is written for one: setup_inputs(seed, part) draws one part's arguments, and reference() takes and returns one part's arrays. A program takes and returns all parts, laid end to end along the dimension named above; each array names one. Nothing has to cross between parts.
Inputs may be any that keep to these rules, and one draw needn't show every extreme that they name: Entries j * 7 to (j + 1) * 7 - 1 of each row of child_map name tiles held by device j of the front's grid, j = grid row * 8 + grid column, that device holding tile rows of its 2048 rows and tile columns of its 1024 columns.
All inputs are finite; a program needn't handle non-finite values.
Results may differ from the reference program's by a relative error of at most 0.0062.
Values may be sent and summed in bfloat16 or wider, within the bound.
A program may use at most 128 MiB of HBM per device.

```python
import jax
import jax.numpy as jnp
from jax import lax

ORDER = 8192
TILE = 128
PANEL = 512
PANELS = 2
SLOTS = 7
NT = 64
GRID_ROWS = 4
GRID_COLS = 8
GROUPS = 32


def draw_child_map(key, part):
    groups = GRID_ROWS * GRID_COLS
    tile_rows = NT // GRID_ROWS
    tile_cols = NT // GRID_COLS
    local_tile = jax.random.randint(key, (groups, groups, SLOTS), 0, tile_rows * tile_cols)
    local_tile = local_tile.at[0, :, 0].set(0)
    local_tile = local_tile.at[groups - 1, :, SLOTS - 1].set(tile_rows * tile_cols - 1)
    target = jnp.arange(groups)[None, :, None]
    grid_row = target // GRID_COLS * tile_rows + local_tile // tile_cols
    grid_col = target % GRID_COLS * tile_cols + local_tile % tile_cols
    return (grid_row * NT + grid_col).reshape(groups, groups * SLOTS).astype(jnp.int32)


def plant(drawn, rng, least, largest):
    extent = drawn.shape
    place = [jax.random.randint(jax.random.fold_in(rng, axis), (), 0, extent[axis]) for axis in range(len(extent))]
    drawn = drawn.at[tuple(place)].set(least)
    longest = extent.index(max(extent))
    place[longest] = (place[longest] + 1) % extent[longest]
    return drawn.at[tuple(place)].set(largest)


def level_of(stream_key, shape, split, least, top_value):
    gain = 1.0
    for position, blocks in split:
        draws = jax.random.uniform(jax.random.fold_in(jax.random.fold_in(stream_key, 6), position), (blocks,), jnp.float32, least / len(split), top_value / len(split))
        gain = gain * jnp.repeat(jnp.exp(draws), shape[position] // blocks).reshape((-1,) + (1,) * (len(shape) - 1 - position))
    return gain


def normal_values(stream_key, dims, width, limit, pieces=(), dtype=jnp.bfloat16):
    gain = level_of(stream_key, dims, pieces, -0.22, 0.18) if pieces else 1.0
    entries = jax.random.normal(stream_key, dims, jnp.float32) * width * gain
    return jnp.minimum(jnp.maximum(entries, -limit), limit).astype(dtype)


def setup_inputs(seed: int = 0, part: int = 0) -> dict:
    keys = jax.random.split(jax.random.key(seed), 6)
    part_keys = jax.random.split(jax.random.fold_in(keys[5], part), 6)
    return {
        "front_in": normal_values(part_keys[0], (ORDER, ORDER), 1.0, 6.0, ((0, 4), (1, 8)), jnp.float32),
        "child_tiles": normal_values(part_keys[1], (GROUPS, GROUPS * SLOTS, TILE, TILE), 1.0, 6.0, ((0, 32),)),
        "child_map": draw_child_map(jax.random.fold_in(jax.random.fold_in(keys[5], part), 71), part),
        "pattern": plant((jax.random.randint(part_keys[3], (NT, NT), 0, 4) < 3).astype(jnp.int32), jax.random.fold_in(part_keys[3], 1), 0, 1),
        "pivot_inverse": normal_values(part_keys[4], (PANELS, PANEL, PANEL), (PANEL * PANEL) ** -0.5, 0.01171875, (), jnp.float32),
    }


def reference(front_in, child_tiles, child_map, pattern, pivot_inverse):
    child_flat = child_tiles.reshape(-1, TILE, TILE).astype(jnp.float32)
    target = child_map.reshape(-1).astype(jnp.int32)
    grid_row = target // NT
    grid_col = target % NT
    matrix = front_in.reshape(NT, TILE, NT, TILE).at[grid_row, :, grid_col, :].add(child_flat).reshape(ORDER, ORDER)
    for panel_index in range(PANELS):
        first_col = panel_index * PANEL
        finish = first_col + PANEL
        lower_part = jnp.dot(matrix[finish:, first_col:finish], pivot_inverse[panel_index], precision=lax.Precision.HIGHEST, preferred_element_type=jnp.float32)
        upper_rows = matrix[first_col:finish, finish:].astype(jnp.bfloat16)
        update = jnp.dot(lower_part.astype(jnp.bfloat16), upper_rows, preferred_element_type=jnp.float32)
        tile_mask = pattern[finish // TILE:, finish // TILE:].astype(jnp.float32)
        count = NT - finish // TILE
        update = (update.reshape(count, TILE, count, TILE) * tile_mask[:, None, :, None]).reshape(count * TILE, count * TILE)
        matrix = matrix.at[finish:, finish:].add(-update)
        matrix = matrix.at[finish:, first_col:finish].set(lower_part)
    return matrix
```

```python
import functools

import jax
import jax.numpy as jnp
from jax import lax
from jax.experimental import pallas as pl
from jax.experimental.pallas import tpu as pltpu
from jax.sharding import PartitionSpec as P

TILE = 128
PANEL = 512
SLOTS = 7
NT = 64
ROWS = 2048
COLS = 1024
MESH = pl.DeviceIdType.MESH
ANY = pl.BlockSpec(memory_space=pl.ANY)
VMEM = pl.BlockSpec(memory_space=pltpu.VMEM)
SMEM = pl.BlockSpec(memory_space=pltpu.SMEM)
F32 = jnp.float32
BF16 = jnp.bfloat16


def position():
    col = lax.axis_index("col")
    return lax.axis_index("front"), lax.axis_index("row"), col // 2, lax.rem(col, 2)


def mod4(v):
    return lax.rem(v + 8, 4)


def device(x, y, z, k):
    return (x, mod4(y), mod4(z) * 2 + k)


def remote(src, dst, send, recv, to):
    return pltpu.make_async_remote_copy(src, dst, send, recv, device_id=to, device_id_type=MESH)


def greet(peers):
    barrier = pltpu.get_barrier_semaphore()
    for peer in peers:
        pl.semaphore_signal(barrier, inc=1, device_id=peer, device_id_type=MESH)
    pl.semaphore_wait(barrier, len(peers))


STEPS = (1, 3, 2)


def exchange_kernel(src, dst, mid, send, recv, local):
    x, y, z, k = position()
    other = 1 - k
    greet(
        [device(x, y + d, z, c) for d in STEPS for c in (k, other)]
        + [device(x, y, z + d, c) for d in STEPS for c in (k, other)]
        + [device(x, y, z, other)]
    )
    count = 0

    def send_to(block, target, to):
        nonlocal count
        copy = remote(block, target, send.at[count], recv.at[count], to)
        copy.start()
        count += 1
        return copy

    first = []
    for a in STEPS:
        for b in STEPS:
            first.append(
                (
                    send_to(src.at[mod4(y + a), mod4(z + b), k], mid.at[0, a, b], device(x, y + a, z, k)),
                    send_to(
                        src.at[mod4(y + b), mod4(z + a), other], mid.at[1, a, b], device(x, y, z + a, other)
                    ),
                    a,
                    b,
                )
            )
    rest = []
    for d in STEPS:
        rest.append(send_to(src.at[mod4(y + d), z, k], dst.at[y, z, k], device(x, y + d, z, k)))
        rest.append(send_to(src.at[y, mod4(z + d), k], dst.at[y, z, k], device(x, y, z + d, k)))
        rest.append(send_to(src.at[mod4(y + d), z, other], dst.at[y, z, k], device(x, y + d, z, other)))
        rest.append(send_to(src.at[y, mod4(z + d), other], dst.at[y, z, k], device(x, y, z + d, other)))
    rest.append(send_to(src.at[y, z, other], dst.at[y, z, k], device(x, y, z, other)))
    own = pltpu.make_async_copy(src.at[y, z, k], dst.at[y, z, k], local)
    own.start()
    for by_row, by_col, a, b in first:
        by_row.wait_recv()
        rest.append(send_to(mid.at[0, a, b], dst.at[mod4(y - a), z, k], device(x, y, z + b, k)))
        by_col.wait_recv()
        rest.append(send_to(mid.at[1, a, b], dst.at[y, mod4(z - a), other], device(x, y + b, z, k)))
    for by_row, by_col, _, _ in first:
        by_row.wait_send()
        by_col.wait_send()
    own.wait()
    for copy in rest:
        copy.wait()


def exchange(tiles):
    shape = (4, 4, 2, SLOTS, TILE, TILE)
    copies = 18 + 13 + 18
    return pl.pallas_call(
        exchange_kernel,
        out_shape=(
            jax.ShapeDtypeStruct(shape, tiles.dtype),
            jax.ShapeDtypeStruct((2, 4, 4, SLOTS, TILE, TILE), tiles.dtype),
        ),
        in_specs=[ANY],
        out_specs=(ANY, ANY),
        scratch_shapes=[
            pltpu.SemaphoreType.DMA((copies,)),
            pltpu.SemaphoreType.DMA((copies,)),
            pltpu.SemaphoreType.DMA,
        ],
        compiler_params=pltpu.CompilerParams(collective_id=0, has_side_effects=True),
        name="exchange",
    )(tiles.reshape(shape))[0]


def split(x):
    high = x.astype(BF16)
    return high, (x - high.astype(F32)).astype(BF16)


def wide_dot(a, b):
    a_high, a_low = split(a)
    b_high, b_low = split(b)
    dot = functools.partial(jnp.dot, preferred_element_type=F32)
    return dot(a_high, b_high) + (dot(a_low, b_high) + dot(a_high, b_low))


KIDS = 28


def assemble_kernel(target, front, kids, inverse, full, lower, upper, acc, kid_buf, inv, low, up, sems):
    row = lax.axis_index("row")
    col = lax.axis_index("col")
    groups = 224 // KIDS
    loads = [
        pltpu.make_async_copy(
            front.at[pl.ds(256 * i, 256)], acc.at[pl.ds(256 * i, 256)], sems.at[i]
        )
        for i in range(8)
    ]
    kid_loads = [
        pltpu.make_async_copy(kids.at[pl.ds(KIDS * i, KIDS)], kid_buf.at[pl.ds(KIDS * i, KIDS)], sems.at[8 + i])
        for i in range(groups)
    ]
    for copy in loads + kid_loads:
        copy.start()
    inv_load = pltpu.make_async_copy(inverse.at[0], inv, sems.at[16])
    inv_load.start()
    for copy in loads:
        copy.wait()
    for g in range(groups):
        kid_loads[g].wait()

        def add(i, _):
            t = target[i]
            r = pl.multiple_of((t // 8) * TILE, TILE)
            c = pl.multiple_of(lax.rem(t, 8) * TILE, TILE)
            acc[pl.ds(r, TILE), pl.ds(c, TILE)] += kid_buf[i].astype(F32)
            return 0

        lax.fori_loop(KIDS * g, KIDS * (g + 1), add, 0, unroll=2)
    inv_load.wait()
    right = pltpu.make_async_copy(acc.at[:, pl.ds(PANEL, PANEL)], full.at[:, pl.ds(PANEL, PANEL)], sems.at[0])
    right.start()

    up[...] = acc[0:PANEL, :].astype(BF16)
    up_out = pltpu.make_async_copy(up, upper, sems.at[3])
    up_out.start()

    @pl.when(col == 0)
    def _():
        @pl.loop(0, ROWS // 256)
        def _(i):
            rows = pl.ds(pl.multiple_of(i * 256, 256), 256)
            part = wide_dot(acc[rows, 0:PANEL], inv[...])
            low[rows, :] = part.astype(BF16)

            @pl.when((row > 0) | (i >= 2))
            def _():
                acc[rows, 0:PANEL] = part

    left = pltpu.make_async_copy(acc.at[:, pl.ds(0, PANEL)], full.at[:, pl.ds(0, PANEL)], sems.at[1])
    left.start()
    low_out = pltpu.make_async_copy(low, lower, sems.at[2])
    low_out.start()
    for copy in (right, left, low_out, up_out):
        copy.wait()


def assemble(target, front, kids, inverse):
    return pl.pallas_call(
        assemble_kernel,
        out_shape=(
            jax.ShapeDtypeStruct((ROWS, COLS), F32),
            jax.ShapeDtypeStruct((ROWS, PANEL), BF16),
            jax.ShapeDtypeStruct((PANEL, COLS), BF16),
        ),
        in_specs=[SMEM, ANY, ANY, ANY],
        out_specs=(ANY, ANY, ANY),
        scratch_shapes=[
            pltpu.VMEM((ROWS, COLS), F32),
            pltpu.VMEM((224, TILE, TILE), BF16),
            pltpu.VMEM((PANEL, PANEL), F32),
            pltpu.VMEM((ROWS, PANEL), BF16),
            pltpu.VMEM((PANEL, COLS), BF16),
            pltpu.SemaphoreType.DMA((17,)),
        ],
        compiler_params=pltpu.CompilerParams(vmem_limit_bytes=40 << 20),
        name="assemble",
    )(target, front, kids, inverse)


PIECES = 8


def lower_piece(ref, panel, way, i):
    chunk = lax.rem(i // 2 + 1, 4) * 4 + 2 * way + lax.rem(i, 2)
    return ref.at[pl.ds(pl.multiple_of(chunk * 128, 128), 128), pl.ds(panel * PANEL, PANEL)]


def upper_piece(ref, panel, way, i):
    chunk = lax.rem(i // 4 * 4 + 4, 8) + 2 * way + lax.rem(i, 4) // 2
    start = panel * PANEL + lax.rem(i, 2) * 256
    return ref.at[
        pl.ds(pl.multiple_of(start, 256), 256), pl.ds(pl.multiple_of(chunk * TILE, TILE), TILE)
    ]


def share_kernel(
    full, low_in, up_in, inverse, mask, full_out, low, up,
    panel_cols, panel_rows, inv, part, send_low, recv_low, send_core, send_up, recv_up, sems
):
    x, y, z, k = position()
    other = 1 - k
    first_row = y == 0
    first_col = (z == 0) & (k == 0)
    right = device(x, y, z + 1, k), device(x, y, z - 1, k)
    down = device(x, y + 1, z, k), device(x, y - 1, z, k)
    across = device(x, y, z, other)
    low_hops = z, mod4(-z)
    up_hops = y, mod4(-y)
    loads = [
        pltpu.make_async_copy(full.at[:, pl.ds(PANEL, PANEL)], panel_cols, sems.at[0]),
        pltpu.make_async_copy(full.at[pl.ds(PANEL, PANEL), :], panel_rows, sems.at[1]),
        pltpu.make_async_copy(inverse.at[1], inv, sems.at[2]),
    ]

    for copy in loads:
        copy.start()

    @pl.when(first_col)
    def _():
        copy = pltpu.make_async_copy(low_in, low.at[:, pl.ds(0, PANEL)], sems.at[3])
        copy.start()
        copy.wait()

    @pl.when(first_row)
    def _():
        copy = pltpu.make_async_copy(up_in, up.at[pl.ds(0, PANEL)], sems.at[4])
        copy.start()
        copy.wait()

    greet([*right, *down, across])

    def low_copy(panel, way, i):
        n = (panel * 2 + way) * PIECES + i
        piece = lower_piece(low, panel, way, i)
        return remote(piece, piece, send_low.at[n], recv_low.at[n], right[way])

    def core_copy(panel, way, i):
        n = (panel * 2 + way) * PIECES + i
        piece = lower_piece(low, panel, way, i)
        return remote(piece, piece, send_core.at[n], recv_low.at[n], across)

    def up_copy(panel, way, i):
        n = (panel * 2 + way) * PIECES + i
        piece = upper_piece(up, panel, way, i)
        return remote(piece, piece, send_up.at[n], recv_up.at[n], down[way])

    def phase(panel):
        @pl.loop(0, PIECES + 4)
        def _(t):
            for way in (0, 1):
                i = t - up_hops[way]

                @pl.when((i >= 0) & (i < PIECES))
                def _():
                    @pl.when(y != 0)
                    def _():
                        up_copy(panel, way, i).wait_recv()

                    @pl.when(up_hops[way] < 3)
                    def _():
                        up_copy(panel, way, i).start()

                j = t - low_hops[way] - k

                @pl.when((j >= 0) & (j < PIECES))
                def _():
                    @pl.when(jnp.logical_not(first_col))
                    def _():
                        low_copy(panel, way, j).wait_recv()

                    @pl.when((k == 0) & (low_hops[way] < 3))
                    def _():
                        low_copy(panel, way, j).start()

                    @pl.when(k == 0)
                    def _():
                        core_copy(panel, way, j).start()

    phase(0)
    for copy in loads:
        copy.wait()

    @pl.when(first_row)
    def _():
        for n in range(PANEL // TILE):
            rows = slice(n * TILE, (n + 1) * TILE)
            cut = jnp.dot(
                low[PANEL + n * TILE : PANEL + (n + 1) * TILE, 0:PANEL], up[0:PANEL, :], preferred_element_type=F32
            )
            value = panel_rows[rows, :] - cut * mask[4 + n : 5 + n, :]

            @pl.when(first_col)
            def _():
                panel_rows[rows, PANEL:] = value[:, PANEL:]

            @pl.when(jnp.logical_not(first_col))
            def _():
                panel_rows[rows, :] = value

            up[PANEL + n * TILE : PANEL + (n + 1) * TILE, :] = value.astype(BF16)

    @pl.when(first_col)
    def _():
        for n in range(ROWS // TILE):
            rows = slice(n * TILE, (n + 1) * TILE)
            cut = jnp.dot(low[rows, 0:PANEL], up[0:PANEL, PANEL:], preferred_element_type=F32)
            value = panel_cols[rows, :] - cut * mask[n : n + 1, PANEL:]
            part[rows, :] = wide_dot(value, inv[...])
            low[rows, PANEL:] = part[rows, :].astype(BF16)
    phase(1)

    @pl.when(first_col)
    def _():
        @pl.when(first_row)
        def _():
            copy = pltpu.make_async_copy(
                part.at[pl.ds(2 * PANEL, ROWS - 2 * PANEL)],
                full_out.at[pl.ds(2 * PANEL, ROWS - 2 * PANEL), pl.ds(PANEL, PANEL)],
                sems.at[0],
            )
            copy.start()
            copy.wait()

        @pl.when(jnp.logical_not(first_row))
        def _():
            copy = pltpu.make_async_copy(part, full_out.at[:, pl.ds(PANEL, PANEL)], sems.at[0])
            copy.start()
            copy.wait()

    @pl.when(first_row)
    def _():
        copy = pltpu.make_async_copy(panel_rows, full_out.at[pl.ds(PANEL, PANEL)], sems.at[1])
        copy.start()
        copy.wait()

    @pl.loop(0, PIECES)
    def _(i):
        for panel in (0, 1):
            for way in (0, 1):
                @pl.when(up_hops[way] < 3)
                def _():
                    up_copy(panel, way, i).wait_send()

                @pl.when((k == 0) & (low_hops[way] < 3))
                def _():
                    low_copy(panel, way, i).wait_send()

                @pl.when(k == 0)
                def _():
                    core_copy(panel, way, i).wait_send()


def share(full, low, up, inverse, mask):
    pieces = 2 * 2 * PIECES
    dma = pltpu.SemaphoreType.DMA((pieces,))
    return pl.pallas_call(
        share_kernel,
        out_shape=(
            jax.ShapeDtypeStruct((ROWS, COLS), F32),
            jax.ShapeDtypeStruct((ROWS, 2 * PANEL), BF16),
            jax.ShapeDtypeStruct((2 * PANEL, COLS), BF16),
        ),
        in_specs=[ANY, ANY, ANY, ANY, VMEM],
        out_specs=(ANY, VMEM, VMEM),
        scratch_shapes=[
            pltpu.VMEM((ROWS, PANEL), F32),
            pltpu.VMEM((PANEL, COLS), F32),
            pltpu.VMEM((PANEL, PANEL), F32),
            pltpu.VMEM((ROWS, PANEL), F32),
            dma,
            dma,
            dma,
            dma,
            dma,
            pltpu.SemaphoreType.DMA((5,)),
        ],
        input_output_aliases={0: 0},
        compiler_params=pltpu.CompilerParams(
            collective_id=1, has_side_effects=True, vmem_limit_bytes=48 << 20
        ),
        name="share",
    )(full, low, up, inverse, mask)


BLOCK = 256


def update_kernel(full, low, up, mask, out):
    skip = (lax.axis_index("col") == 0) | (
        (lax.axis_index("row") == 0) & (pl.program_id(0) < 2 * PANEL // BLOCK)
    )

    @pl.when(skip)
    def _():
        out[...] = full[...]

    @pl.when(jnp.logical_not(skip))
    def _():
        for n in range(BLOCK // TILE):
            rows = slice(n * TILE, (n + 1) * TILE)
            cut = jnp.dot(low[rows, :], up[...], preferred_element_type=F32)
            tile_row = pl.program_id(0) * (BLOCK // TILE) + n
            out[rows, :] = full[rows, :] - cut * mask[pl.ds(tile_row, 1), :]


def update(full, low, up, mask):
    return pl.pallas_call(
        update_kernel,
        out_shape=jax.ShapeDtypeStruct((ROWS, COLS), F32),
        grid=(ROWS // BLOCK,),
        in_specs=[
            pl.BlockSpec((BLOCK, COLS), lambda i: (i, 0)),
            pl.BlockSpec((BLOCK, 2 * PANEL), lambda i: (i, 0)),
            pl.BlockSpec((2 * PANEL, COLS), lambda i: (0, 0), pipeline_mode=pl.Buffered(1)),
            pl.BlockSpec((ROWS // TILE, COLS), lambda i: (0, 0), pipeline_mode=pl.Buffered(1)),
        ],
        out_specs=pl.BlockSpec((BLOCK, COLS), lambda i: (i, 0)),
        compiler_params=pltpu.CompilerParams(
            dimension_semantics=("arbitrary",), vmem_limit_bytes=32 << 20
        ),
        name="update",
    )(full, low, up, mask)


def body(front_in, child_tiles, child_map, pattern, pivot_inverse):
    row = lax.axis_index("row")
    col = lax.axis_index("col")
    tile_rows, tile_cols = ROWS // TILE, COLS // TILE
    placed = lax.all_to_all(
        child_map.reshape(32, SLOTS), ("row", "col"), split_axis=0, concat_axis=0, tiled=True
    ).reshape(-1)
    target = (placed // NT - row * tile_rows) * tile_cols + placed % NT - col * tile_cols
    mask = lax.dynamic_slice(
        pattern, (row * tile_rows, col * tile_cols), (tile_rows, tile_cols)
    ).astype(F32)
    mask = jnp.repeat(mask, TILE, axis=1)
    kids = exchange(child_tiles).reshape(-1, TILE, TILE)
    full, low, up = assemble(target, front_in, kids, pivot_inverse)
    full, low, up = share(full, low, up, pivot_inverse, mask)
    return update(full, low, up, mask)


def solution(mesh):
    return jax.shard_map(
        body,
        mesh=mesh,
        in_specs=(
            P(("front", "row"), "col"),
            P(("front", "row", "col"), None, None, None),
            P(("front", "row", "col"), None),
            P("front", None),
            P("front", None, None),
        ),
        out_specs=P(("front", "row"), "col"),
        check_vma=False,
    )
```

```python
import functools

import jax
import jax.numpy as jnp
from jax import lax
from jax.experimental import pallas as pl
from jax.experimental.pallas import tpu as pltpu
from jax.sharding import PartitionSpec as P

TILE = 128
PANEL = 512
SLOTS = 7
NT = 64
ROWS = 2048
COLS = 1024
MESH = pl.DeviceIdType.MESH
ANY = pl.BlockSpec(memory_space=pl.ANY)
VMEM = pl.BlockSpec(memory_space=pltpu.VMEM)
SMEM = pl.BlockSpec(memory_space=pltpu.SMEM)
HBM = pl.BlockSpec(memory_space=pltpu.HBM)
F32 = jnp.float32
BF16 = jnp.bfloat16
SCOPED = 20 << 20


def position():
    col = lax.axis_index("col")
    return lax.axis_index("front"), lax.axis_index("row"), col // 2, lax.rem(col, 2)


def mod4(v):
    return lax.rem(v + 8, 4)


def device(x, y, z, k):
    return (x, mod4(y), mod4(z) * 2 + k)


def remote(src, dst, send, recv, to):
    return pltpu.make_async_remote_copy(src, dst, send, recv, device_id=to, device_id_type=MESH)


def greet(peers):
    barrier = pltpu.get_barrier_semaphore()
    for peer in peers:
        pl.semaphore_signal(barrier, inc=1, device_id=peer, device_id_type=MESH)
    pl.semaphore_wait(barrier, len(peers))


STEPS = (1, 3, 2)


def exchange_kernel(src, own_map, front, dst, maps, acc, mid, send, recv, map_send, map_recv, local):
    x, y, z, k = position()
    other = 1 - k
    me = y * 8 + z * 2 + k

    def partner(d):
        to = lax.rem(me + d, 32)
        return x, to // 8, lax.rem(to, 8)

    greet([partner(d) for d in range(1, 32)])
    count = 0

    def send_to(block, target, to):
        nonlocal count
        copy = remote(block, target, send.at[count], recv.at[count], to)
        copy.start()
        count += 1
        return copy

    first = []
    for a in STEPS:
        for b in STEPS:
            first.append(
                (
                    send_to(src.at[mod4(y + a), mod4(z + b), k], mid.at[0, a, b], device(x, y + a, z, k)),
                    send_to(
                        src.at[mod4(y + b), mod4(z + a), other], mid.at[1, a, b], device(x, y, z + a, other)
                    ),
                    a,
                    b,
                )
            )

    def map_copy(d):
        return remote(own_map, maps.at[me], map_send.at[d], map_recv.at[d], partner(d))

    @pl.loop(1, 32)
    def _(d):
        map_copy(d).start()

    rest = []
    for d in STEPS:
        rest.append(send_to(src.at[mod4(y + d), z, k], dst.at[y, z, k], device(x, y + d, z, k)))
        rest.append(send_to(src.at[y, mod4(z + d), k], dst.at[y, z, k], device(x, y, z + d, k)))
        rest.append(send_to(src.at[mod4(y + d), z, other], dst.at[y, z, k], device(x, y + d, z, other)))
        rest.append(send_to(src.at[y, mod4(z + d), other], dst.at[y, z, k], device(x, y, z + d, other)))
    rest.append(send_to(src.at[y, z, other], dst.at[y, z, k], device(x, y, z, other)))
    own = [
        pltpu.make_async_copy(src.at[y, z, k], dst.at[y, z, k], local.at[0]),
        pltpu.make_async_copy(own_map, maps.at[me], local.at[1]),
        pltpu.make_async_copy(front, acc, local.at[2]),
    ]
    for copy in own:
        copy.start()
    for by_row, by_col, a, b in first:
        by_row.wait_recv()
        rest.append(send_to(mid.at[0, a, b], dst.at[mod4(y - a), z, k], device(x, y, z + b, k)))
        by_col.wait_recv()
        rest.append(send_to(mid.at[1, a, b], dst.at[y, mod4(z - a), other], device(x, y + b, z, k)))
    for by_row, by_col, _, _ in first:
        by_row.wait_send()
        by_col.wait_send()
    for copy in own:
        copy.wait()

    @pl.loop(1, 32)
    def _(d):
        map_copy(d).wait()

    for copy in rest:
        copy.wait()


def exchange(tiles, child_map, front):
    shape = (4, 4, 2, SLOTS, TILE, TILE)
    copies = 18 + 13 + 18
    return pl.pallas_call(
        exchange_kernel,
        out_shape=(
            pltpu.VMEM(shape, tiles.dtype),
            jax.ShapeDtypeStruct((32, *child_map.shape), child_map.dtype),
            pltpu.VMEM(front.shape, front.dtype),
            jax.ShapeDtypeStruct((2, 4, 4, SLOTS, TILE, TILE), tiles.dtype),
        ),
        in_specs=[HBM, HBM, HBM],
        out_specs=(VMEM, ANY, VMEM, HBM),
        scratch_shapes=[
            pltpu.SemaphoreType.DMA((copies,)),
            pltpu.SemaphoreType.DMA((copies,)),
            pltpu.SemaphoreType.DMA((32,)),
            pltpu.SemaphoreType.DMA((32,)),
            pltpu.SemaphoreType.DMA((3,)),
        ],
        compiler_params=pltpu.CompilerParams(
            collective_id=0, has_side_effects=True, vmem_limit_bytes=SCOPED
        ),
        name="exchange",
    )(*(pltpu.with_memory_space_constraint(v, pltpu.HBM) for v in (tiles.reshape(shape), child_map, front)))[:3]


def split(x):
    high = x.astype(BF16)
    return high, (x - high.astype(F32)).astype(BF16)


def wide_dot(a, b_high, b_low):
    a_high, a_low = split(a)
    dot = functools.partial(jnp.dot, preferred_element_type=F32)
    return dot(a_high, b_high) + (dot(a_low, b_high) + dot(a_high, b_low))


def assemble_kernel(maps, kids, front, full):
    row = lax.axis_index("row")
    col = lax.axis_index("col")
    first = (row * 8 + col) * SLOTS

    @pl.loop(0, 32)
    def _(source):
        for slot in range(SLOTS):
            t = maps[source, 0, first + slot]
            r = pl.multiple_of((t // NT - row * 16) * TILE, TILE)
            c = pl.multiple_of((lax.rem(t, NT) - col * 8) * TILE, TILE)
            full[pl.ds(r, TILE), pl.ds(c, TILE)] += kids[source * SLOTS + slot].astype(F32)


def assemble(maps, kids, front):
    return pl.pallas_call(
        assemble_kernel,
        out_shape=pltpu.VMEM((ROWS, COLS), F32),
        in_specs=[SMEM, VMEM, VMEM],
        out_specs=VMEM,
        input_output_aliases={2: 0},
        compiler_params=pltpu.CompilerParams(vmem_limit_bytes=SCOPED),
        name="assemble",
    )(maps, kids, front)


PIECES = 8
WINDOW = 3
SKEW = 2
GAP = 2 * (SKEW - 1)


def lower_chunk(way, i):
    return lax.rem(i // 2 + 1, 4) * 4 + 2 * way + lax.rem(i, 2)


def upper_chunk(way, i):
    return lax.rem(i // 4 * 4 + 4, 8) + 2 * way + lax.rem(i, 4) // 2, lax.rem(i, 2)


def rows_of(chunk, count):
    return pl.ds(pl.multiple_of(chunk * count, count), count)


def share_kernel(
    full, inverse, pattern, low, up, mat, pivot_rows,
    inv, inv_high, inv_low, send_low, recv_low, send_core, send_up, recv_up, sem
):
    x, y, z, k = position()
    first_row = y == 0
    first_col = (z == 0) & (k == 0)
    right = device(x, y, z + 1, k), device(x, y, z - 1, k)
    down = device(x, y + 1, z, k), device(x, y - 1, z, k)
    across = device(x, y, z, 1 - k)
    low_hops = z, mod4(-z)
    up_hops = y, mod4(-y)

    def kept(chunk, tile_col):
        return pattern[y * 16 + chunk, (z * 2 + k) * 8 + tile_col].astype(F32)

    seeds = first_row & jnp.logical_not(first_col)
    inv_load = pltpu.make_async_copy(inverse, inv, sem)

    @pl.when(first_col)
    def _():
        inv_load.start()

    @pl.when(first_row)
    def _():
        up[0:PANEL, :] = full[0:PANEL, :].astype(BF16)

    @pl.when(first_col)
    def _():
        inv_load.wait()
        high, rest = split(inv[...])
        inv_high[...] = high
        inv_low[...] = rest

    greet([*right, *down, across])

    def low_piece(way, g):
        panel, i = g // PIECES, lax.rem(g, PIECES)
        return low.at[rows_of(lower_chunk(way, i), TILE), pl.ds(pl.multiple_of(panel * PANEL, PANEL), PANEL)]

    def low_copy(way, g):
        n = way * 2 * PIECES + g
        piece = low_piece(way, g)
        return remote(piece, piece, send_low.at[n], recv_low.at[n], right[way])

    def core_copy(way, g):
        n = way * 2 * PIECES + g
        piece = low_piece(way, g)
        return remote(piece, piece, send_core.at[n], recv_low.at[n], across)

    def up_copy(way, g):
        n = way * 2 * PIECES + g
        panel, i = g // PIECES, lax.rem(g, PIECES)
        chunk, half = upper_chunk(way, i)
        piece = up.at[rows_of(panel * 2 + half, 256), rows_of(chunk, TILE)]
        return remote(piece, piece, send_up.at[n], recv_up.at[n], down[way])

    def make_low(g):
        i = lax.rem(g, PIECES)
        group = lower_chunk(0, i) // 4
        rows = rows_of(group, PANEL)
        solved = (y > 0) | (group >= 1)

        @pl.when(g < PIECES)
        def _():
            part = wide_dot(full[rows, 0:PANEL], inv_high[0], inv_low[0])
            low[rows, 0:PANEL] = part.astype(BF16)
            mat[rows, PANEL:] = full[rows, PANEL:]

            @pl.when(solved)
            def _():
                mat[rows, 0:PANEL] = part

            @pl.when(jnp.logical_not(solved))
            def _():
                mat[rows, 0:PANEL] = full[rows, 0:PANEL]

        @pl.when((g >= PIECES) & solved)
        def _():
            cut = jnp.dot(low[rows, 0:PANEL], up[0:PANEL, PANEL:], preferred_element_type=F32)
            for m in range(4):
                for n in range(4):
                    here = pl.ds(pl.multiple_of(group * PANEL + m * TILE, TILE), TILE)
                    cols = slice(PANEL + n * TILE, PANEL + (n + 1) * TILE)
                    mat[here, cols] -= cut[m * TILE : (m + 1) * TILE, n * TILE : (n + 1) * TILE] * kept(
                        group * 4 + m, 4 + n
                    )
            part = wide_dot(mat[rows, PANEL:], inv_high[1], inv_low[1])
            low[rows, PANEL:] = part.astype(BF16)

            @pl.when((y > 0) | (group >= 2))
            def _():
                mat[rows, PANEL:] = part

        @pl.when((g >= PIECES) & jnp.logical_not(solved))
        def _():
            low[rows, PANEL:] = jnp.zeros((PANEL, PANEL), BF16)

    def make_up(way, g):
        chunk, _ = upper_chunk(way, lax.rem(g, PIECES))
        cols = rows_of(chunk, TILE)
        cut = jnp.dot(low[PANEL : 2 * PANEL, 0:PANEL], up[0:PANEL, cols], preferred_element_type=F32)
        for n in range(4):
            tile = slice(n * TILE, (n + 1) * TILE)
            value = full[PANEL + n * TILE : PANEL + (n + 1) * TILE, cols] - cut[tile] * kept(4 + n, chunk)
            pivot_rows[tile, cols] = value
            up[PANEL + n * TILE : PANEL + (n + 1) * TILE, cols] = value.astype(BF16)

    total = 2 * PIECES

    def due(step):
        late = step >= PIECES + GAP
        return jnp.where(late, step - GAP, step), ((step >= 0) & (step < PIECES)) | (late & (step < total + GAP))

    @pl.loop(0, total + GAP + 3 * SKEW + 1)
    def _(t):
        for way in (0, 1):
            i, here = due(t - SKEW * up_hops[way])

            @pl.when(here)
            def _(way=way, i=i):
                @pl.when(y != 0)
                def _():
                    up_copy(way, i).wait_recv()

                @pl.when(first_row & (i >= PIECES) & (lax.rem(i, 2) == 0))
                def _():
                    make_up(way, i)

                @pl.when(up_hops[way] < 3)
                def _():
                    @pl.when(i >= WINDOW)
                    def _():
                        up_copy(way, i - WINDOW).wait_send()

                    up_copy(way, i).start()

        g, here = due(t)

        @pl.when(first_col & here & (lax.rem(g, 2) == 0))
        def _():
            make_low(g)

        for way in (0, 1):
            j, here = due(t - SKEW * low_hops[way] - k)

            @pl.when(here)
            def _(way=way, j=j):
                @pl.when(jnp.logical_not(first_col))
                def _():
                    low_copy(way, j).wait_recv()

                @pl.when((k == 0) & (low_hops[way] < 3))
                def _():
                    @pl.when(j >= WINDOW)
                    def _():
                        low_copy(way, j - WINDOW).wait_send()

                    low_copy(way, j).start()

                @pl.when(k == 0)
                def _():
                    @pl.when(j >= WINDOW)
                    def _():
                        core_copy(way, j - WINDOW).wait_send()

                    core_copy(way, j).start()

    for way in (0, 1):
        for i in range(total - WINDOW, total):
            @pl.when(up_hops[way] < 3)
            def _():
                up_copy(way, i).wait_send()

            @pl.when((k == 0) & (low_hops[way] < 3))
            def _():
                low_copy(way, i).wait_send()

            @pl.when(k == 0)
            def _():
                core_copy(way, i).wait_send()


def share(full, inverse, pattern):
    dma = pltpu.SemaphoreType.DMA((2 * 2 * PIECES,))
    return pl.pallas_call(
        share_kernel,
        out_shape=(
            pltpu.VMEM((ROWS, 2 * PANEL), BF16),
            pltpu.VMEM((2 * PANEL, COLS), BF16),
            pltpu.VMEM((ROWS, COLS), F32),
            pltpu.VMEM((PANEL, COLS), F32),
        ),
        in_specs=[VMEM, ANY, SMEM],
        out_specs=(VMEM, VMEM, VMEM, VMEM),
        scratch_shapes=[
            pltpu.VMEM((2, PANEL, PANEL), F32),
            pltpu.VMEM((2, PANEL, PANEL), BF16),
            pltpu.VMEM((2, PANEL, PANEL), BF16),
            dma,
            dma,
            dma,
            dma,
            dma,
            pltpu.SemaphoreType.DMA,
        ],
        compiler_params=pltpu.CompilerParams(
            collective_id=1, has_side_effects=True, vmem_limit_bytes=SCOPED
        ),
        name="share",
    )(full, inverse, pattern)


BLOCK = 512


def update_kernel(pattern, full, low, up, mat, pivot_rows, out, slots, sems):
    row = lax.axis_index("row")
    col = lax.axis_index("col")
    first_col = col == 0
    first_row = row == 0

    def store(source, block):
        return pltpu.make_async_copy(source, out.at[rows_of(block, BLOCK)], sems.at[lax.rem(block, 2)])

    @pl.when(first_col)
    def _():
        copy = pltpu.make_async_copy(mat, out, sems.at[2])
        copy.start()
        copy.wait()

    @pl.when(jnp.logical_not(first_col))
    def _():
        start = jnp.where(first_row, 2, 0)
        above = [
            pltpu.make_async_copy(full.at[0:PANEL], out.at[0:PANEL], sems.at[2]),
            pltpu.make_async_copy(pivot_rows, out.at[PANEL : 2 * PANEL], sems.at[3]),
        ]

        @pl.when(first_row)
        def _():
            for copy in above:
                copy.start()

        @pl.loop(start, ROWS // BLOCK)
        def _(block):
            rows = rows_of(block, BLOCK)
            slot = lax.rem(block, 2)

            @pl.when(block >= start + 2)
            def _():
                store(slots.at[slot], block).wait()

            cut = jnp.dot(low[rows, :], up[...], preferred_element_type=F32)
            for m in range(BLOCK // TILE):
                here = pl.ds(pl.multiple_of(block * BLOCK + m * TILE, TILE), TILE)
                tile = slice(m * TILE, (m + 1) * TILE)
                for c in range(COLS // TILE):
                    cols = slice(c * TILE, (c + 1) * TILE)
                    keep = pattern[row * 16 + block * (BLOCK // TILE) + m, col * 8 + c].astype(F32)
                    slots[slot, tile, cols] = full[here, cols] - cut[tile, cols] * keep
            store(slots.at[slot], block).start()

        for block in (2, 3):
            store(slots.at[block % 2], block).wait()

        @pl.when(first_row)
        def _():
            for copy in above:
                copy.wait()


def update(pattern, full, low, up, mat, pivot_rows):
    return pl.pallas_call(
        update_kernel,
        out_shape=jax.ShapeDtypeStruct((ROWS, COLS), F32),
        in_specs=[SMEM, VMEM, VMEM, VMEM, VMEM, VMEM],
        out_specs=ANY,
        scratch_shapes=[pltpu.VMEM((2, BLOCK, COLS), F32), pltpu.SemaphoreType.DMA((4,))],
        compiler_params=pltpu.CompilerParams(vmem_limit_bytes=SCOPED),
        name="update",
    )(pattern, full, low, up, mat, pivot_rows)


def body(front_in, child_tiles, child_map, pattern, pivot_inverse):
    kids, maps, front = exchange(child_tiles, child_map, front_in)
    full = assemble(maps, kids.reshape(-1, TILE, TILE), front)
    low, up, mat, pivot_rows = share(full, pivot_inverse, pattern)
    return update(pattern, full, low, up, mat, pivot_rows)


def solution(mesh):
    return jax.shard_map(
        body,
        mesh=mesh,
        in_specs=(
            P(("front", "row"), "col"),
            P(("front", "row", "col"), None, None, None),
            P(("front", "row", "col"), None),
            P("front", None),
            P("front", None, None),
        ),
        out_specs=P(("front", "row"), "col"),
        check_vma=False,
    )
```

```python
import functools

import jax
import jax.numpy as jnp
from jax import lax
from jax.experimental import pallas as pl
from jax.experimental.pallas import tpu as pltpu
from jax.sharding import PartitionSpec as P

TILE = 128
PANEL = 512
SLOTS = 7
NT = 64
ROWS = 2048
COLS = 1024
MESH = pl.DeviceIdType.MESH
ANY = pl.BlockSpec(memory_space=pl.ANY)
VMEM = pl.BlockSpec(memory_space=pltpu.VMEM)
SMEM = pl.BlockSpec(memory_space=pltpu.SMEM)
HBM = pl.BlockSpec(memory_space=pltpu.HBM)
F32 = jnp.float32
BF16 = jnp.bfloat16
SCOPED = 16 << 20


def position():
    col = lax.axis_index("col")
    return lax.axis_index("front"), lax.axis_index("row"), col // 2, lax.rem(col, 2)


def mod4(v):
    return lax.rem(v + 8, 4)


def device(x, y, z, k):
    return (x, mod4(y), mod4(z) * 2 + k)


def remote(src, dst, send, recv, to):
    return pltpu.make_async_remote_copy(src, dst, send, recv, device_id=to, device_id_type=MESH)


def greet(peers):
    barrier = pltpu.get_barrier_semaphore()
    for peer in peers:
        pl.semaphore_signal(barrier, inc=1, device_id=peer, device_id_type=MESH)
    pl.semaphore_wait(barrier, len(peers))


STEPS = (1, 3, 2)
TURNS = ((1, 3), (3, 1), (2, 2), (3, 3), (1, 1), (2, 1), (1, 2), (3, 2), (2, 3))


def exchange_kernel(src, own_map, front, dst, maps, acc, mid, send, recv, map_send, map_recv, local):
    x, y, z, k = position()
    other = 1 - k
    me = y * 8 + z * 2 + k

    def partner(d):
        to = lax.rem(me + d, 32)
        return x, to // 8, lax.rem(to, 8)

    greet([partner(d) for d in range(1, 32)])
    count = 0

    def send_to(block, target, to):
        nonlocal count
        copy = remote(block, target, send.at[count], recv.at[count], to)
        copy.start()
        count += 1
        return copy

    first = []
    for a, b in TURNS:
        first.append(
            (
                send_to(src.at[mod4(y + a), mod4(z + b), k], mid.at[0, a, b], device(x, y + a, z, k)),
                send_to(src.at[mod4(y + b), mod4(z + a), other], mid.at[1, a, b], device(x, y, z + a, other)),
                a,
                b,
            )
        )

    def map_copy(d):
        return remote(own_map, maps.at[me], map_send.at[d], map_recv.at[d], partner(d))

    @pl.loop(1, 32)
    def _(d):
        map_copy(d).start()

    rest = []
    for d in STEPS:
        rest.append(send_to(src.at[mod4(y + d), z, k], dst.at[y, z, k], device(x, y + d, z, k)))
        rest.append(send_to(src.at[y, mod4(z + d), k], dst.at[y, z, k], device(x, y, z + d, k)))
        rest.append(send_to(src.at[mod4(y + d), z, other], dst.at[y, z, k], device(x, y + d, z, other)))
        rest.append(send_to(src.at[y, mod4(z + d), other], dst.at[y, z, k], device(x, y, z + d, other)))
    rest.append(send_to(src.at[y, z, other], dst.at[y, z, k], device(x, y, z, other)))
    own = [
        pltpu.make_async_copy(src.at[y, z, k], dst.at[y, z, k], local.at[0]),
        pltpu.make_async_copy(own_map, maps.at[me], local.at[1]),
        pltpu.make_async_copy(front, acc, local.at[2]),
    ]
    for copy in own:
        copy.start()
    for by_row, by_col, a, b in first:
        by_row.wait_recv()
        rest.append(send_to(mid.at[0, a, b], dst.at[mod4(y - a), z, k], device(x, y, z + b, k)))
        by_col.wait_recv()
        rest.append(send_to(mid.at[1, a, b], dst.at[y, mod4(z - a), other], device(x, y + b, z, k)))
    for by_row, by_col, _, _ in first:
        by_row.wait_send()
        by_col.wait_send()
    for copy in own:
        copy.wait()

    @pl.loop(1, 32)
    def _(d):
        map_copy(d).wait()

    for copy in rest:
        copy.wait()


def exchange(tiles, child_map, front):
    shape = (4, 4, 2, SLOTS, TILE, TILE)
    copies = 18 + 13 + 18
    return pl.pallas_call(
        exchange_kernel,
        out_shape=(
            pltpu.VMEM(shape, tiles.dtype),
            jax.ShapeDtypeStruct((32, *child_map.shape), child_map.dtype),
            pltpu.VMEM(front.shape, front.dtype),
            jax.ShapeDtypeStruct((2, 4, 4, SLOTS, TILE, TILE), tiles.dtype),
        ),
        in_specs=[HBM, HBM, HBM],
        out_specs=(VMEM, ANY, VMEM, HBM),
        scratch_shapes=[
            pltpu.SemaphoreType.DMA((copies,)),
            pltpu.SemaphoreType.DMA((copies,)),
            pltpu.SemaphoreType.DMA((32,)),
            pltpu.SemaphoreType.DMA((32,)),
            pltpu.SemaphoreType.DMA((3,)),
        ],
        compiler_params=pltpu.CompilerParams(
            collective_id=0, has_side_effects=True, vmem_limit_bytes=SCOPED
        ),
        name="exchange",
    )(*(pltpu.with_memory_space_constraint(v, pltpu.HBM) for v in (tiles.reshape(shape), child_map, front)))[:3]


def split(x):
    high = x.astype(BF16)
    return high, (x - high.astype(F32)).astype(BF16)


def wide_dot(a, b_high, b_low):
    a_high, a_low = split(a)
    dot = functools.partial(jnp.dot, preferred_element_type=F32)
    return dot(a_high, b_high) + (dot(a_low, b_high) + dot(a_high, b_low))


def assemble_kernel(maps, kids, front, full):
    row = lax.axis_index("row")
    col = lax.axis_index("col")
    first = (row * 8 + col) * SLOTS

    @pl.loop(0, 32)
    def _(source):
        for slot in range(SLOTS):
            t = maps[source, 0, first + slot]
            r = pl.multiple_of((t // NT - row * 16) * TILE, TILE)
            c = pl.multiple_of((lax.rem(t, NT) - col * 8) * TILE, TILE)
            full[pl.ds(r, TILE), pl.ds(c, TILE)] += kids[source * SLOTS + slot].astype(F32)


def assemble(maps, kids, front):
    return pl.pallas_call(
        assemble_kernel,
        out_shape=pltpu.VMEM((ROWS, COLS), F32),
        in_specs=[SMEM, VMEM, VMEM],
        out_specs=VMEM,
        input_output_aliases={2: 0},
        compiler_params=pltpu.CompilerParams(vmem_limit_bytes=SCOPED),
        name="assemble",
    )(maps, kids, front)


PART = 2
PIECES = 4 * PART
WINDOW = 3
SKEW = 3
LEAD = 2
GAP = max(0, 3 * SKEW + LEAD + PART - 1 - PIECES)


def rows_of(chunk, count):
    return pl.ds(pl.multiple_of(chunk * count, count), count)


def lower_group(i):
    return lax.rem(i // PART + 1, 4)


def upper_chunk(way, i):
    q = i // PART
    return lax.rem(q // 2 * 4 + 4, 8) + 2 * way + lax.rem(q, 2)


def share_kernel(
    full, inverse, pattern, low, up, mat, pivot_rows,
    inv, inv_high, inv_low, send_low, recv_low, send_core, send_up, recv_up, send_corner, recv_corner, sem
):
    x, y, z, k = position()
    first_row = y == 0
    first_col = (z == 0) & (k == 0)
    down = device(x, y + 1, z, k), device(x, y - 1, z, k)
    across = device(x, y, z, 1 - k)
    ahead = device(x, y, z + 1, 0), device(x, y, z - 1, 1)
    low_hops = z, mod4(-z)
    up_hops = y, mod4(-y)

    def kept(chunk, tile_col):
        return pattern[y * 16 + chunk, (z * 2 + k) * 8 + tile_col].astype(F32)

    seeds = first_row & jnp.logical_not(first_col)
    inv_load = pltpu.make_async_copy(inverse, inv, sem)

    @pl.when(first_col)
    def _():
        inv_load.start()

    @pl.when(first_row)
    def _():
        up[0:PANEL, :] = full[0:PANEL, :].astype(BF16)

    @pl.when(first_col)
    def _():
        inv_load.wait()
        high, rest = split(inv[...])
        inv_high[...] = high
        inv_low[...] = rest

    greet(
        [device(x, y, z + d, c) for d in (1, -1) for c in (k, 1 - k)]
        + [*down, across]
    )

    def low_piece(way, g):
        panel, i = g // PIECES, lax.rem(g, PIECES)
        row = (lower_group(i) * 2 + way) * PART + lax.rem(i, PART)
        return low.at[rows_of(row, 256 // PART), rows_of(panel, PANEL)]

    def low_copy(way, g):
        n = way * 2 * PIECES + g
        piece = low_piece(way, g)
        return remote(piece, piece, send_low.at[n], recv_low.at[n], ahead[way])

    def core_copy(way, g):
        n = way * 2 * PIECES + g
        piece = low_piece(way, g)
        return remote(piece, piece, send_core.at[n], recv_low.at[n], across)

    def up_copy(way, g):
        n = way * 2 * PIECES + g
        panel, i = g // PIECES, lax.rem(g, PIECES)
        piece = up.at[
            rows_of(panel * PART + lax.rem(i, PART), PANEL // PART), rows_of(upper_chunk(way, i), TILE)
        ]
        return remote(piece, piece, send_up.at[n], recv_up.at[n], down[way])

    def make_low(g):
        group = lower_group(lax.rem(g, PIECES))
        rows = rows_of(group, PANEL)
        solved = (y > 0) | (group >= 1)

        @pl.when(g < PIECES)
        def _():
            part = wide_dot(full[rows, 0:PANEL], inv_high[0], inv_low[0])
            low[rows, 0:PANEL] = part.astype(BF16)
            mat[rows, PANEL:] = full[rows, PANEL:]

            @pl.when(solved)
            def _():
                mat[rows, 0:PANEL] = part

            @pl.when(jnp.logical_not(solved))
            def _():
                mat[rows, 0:PANEL] = full[rows, 0:PANEL]

        @pl.when((g >= PIECES) & solved)
        def _():
            cut = jnp.dot(low[rows, 0:PANEL], up[0:PANEL, PANEL:], preferred_element_type=F32)
            for m in range(4):
                for n in range(4):
                    here = pl.ds(pl.multiple_of(group * PANEL + m * TILE, TILE), TILE)
                    cols = slice(PANEL + n * TILE, PANEL + (n + 1) * TILE)
                    mat[here, cols] -= cut[m * TILE : (m + 1) * TILE, n * TILE : (n + 1) * TILE] * kept(
                        group * 4 + m, 4 + n
                    )
            part = wide_dot(mat[rows, PANEL:], inv_high[1], inv_low[1])
            low[rows, PANEL:] = part.astype(BF16)

            @pl.when((y > 0) | (group >= 2))
            def _():
                mat[rows, PANEL:] = part

        @pl.when((g >= PIECES) & jnp.logical_not(solved))
        def _():
            low[rows, PANEL:] = jnp.zeros((PANEL, PANEL), BF16)

    def make_up(way, g):
        chunk = upper_chunk(way, lax.rem(g, PIECES))
        cols = rows_of(chunk, TILE)
        cut = jnp.dot(low[PANEL : 2 * PANEL, 0:PANEL], up[0:PANEL, cols], preferred_element_type=F32)
        for n in range(4):
            tile = slice(n * TILE, (n + 1) * TILE)
            value = full[PANEL + n * TILE : PANEL + (n + 1) * TILE, cols] - cut[tile] * kept(4 + n, chunk)
            pivot_rows[tile, cols] = value
            up[PANEL + n * TILE : PANEL + (n + 1) * TILE, cols] = value.astype(BF16)

    def corner_copy(n, d):
        piece = up.at[rows_of(n, TILE), pl.ds(PANEL, PANEL)]
        slot = n if d > 0 else 4 + n
        return remote(piece, piece, send_corner.at[slot], recv_corner.at[n], device(x, y + d, z, k))

    def pass_corner(n):
        for d in (1, -1):
            @pl.when(y == mod4(d))
            def _(d=d):
                copy = corner_copy(n if d > 0 else 2 + n, d)
                copy.wait_recv()
                copy.start()

    @pl.when(first_row & first_col)
    def _():
        for n in range(2):
            for d, piece in ((1, n), (-1, 2 + n)):
                corner_copy(piece, d).start()
        for n in range(2):
            for d, piece in ((1, 2 + n), (-1, n)):
                corner_copy(piece, d).start()

    total = 2 * PIECES

    def due(step):
        second = step >= PIECES + GAP
        return jnp.where(second, step - GAP, step), ((step >= 0) & (step < PIECES)) | (second & (step < total + GAP))

    def paced(copy_of, way, g):
        @pl.when(g >= WINDOW)
        def _():
            copy_of(way, g - WINDOW).wait_send()

        copy_of(way, g).start()

    def drain(copy_of, way):
        @pl.loop(total - WINDOW, total)
        def _(g):
            copy_of(way, g).wait_send()

    def arrivals(copy_of, way, start, stop):
        @pl.loop(start, stop)
        def _(g):
            copy_of(way, g).wait_recv()

    def hold_low(way):
        return (z != 0) & (k == way)

    @pl.loop(0, total + GAP + 3 * SKEW + LEAD)
    def _(t):
        for way in (0, 1):
            j, here = due(t - SKEW * low_hops[way] - LEAD)

            @pl.when(here & hold_low(way))
            def _(way=way, j=j):
                low_copy(way, j).wait_recv()

                @pl.when(low_hops[way] < 3)
                def _():
                    paced(low_copy, way, j)

                paced(core_copy, way, j)

        for way in (0, 1):
            i, here = due(t - SKEW * up_hops[way] - LEAD)

            @pl.when(here & (y != 0) & (up_hops[way] < 3) & jnp.logical_not(first_col))
            def _(way=way, i=i):
                up_copy(way, i).wait_recv()
                paced(up_copy, way, i)

        g, here = due(t)

        @pl.when(here & seeds)
        def _():
            @pl.when(g == PIECES)
            def _():
                for way in (0, 1):
                    @pl.when(jnp.logical_not(hold_low(way)))
                    def _(way=way):
                        arrivals(low_copy, way, 0, PART)

            for way in (0, 1):
                @pl.when((g >= PIECES) & (lax.rem(g, PART) == 0))
                def _(way=way):
                    make_up(way, g)

                paced(up_copy, way, g)

        @pl.when(here & first_col)
        def _():
            @pl.when(t == 4)
            def _():
                pass_corner(0)

            @pl.when(t == 6)
            def _():
                pass_corner(1)

            @pl.when(g == PIECES)
            def _():
                for n in range(4):
                    @pl.when((y == 2) | ((y == 1) & (n >= 2)) | ((y == 3) & (n < 2)))
                    def _(n=n):
                        corner_copy(n, 1).wait_recv()

            @pl.when(lax.rem(g, PART) == 0)
            def _():
                make_low(g)

            for way in (0, 1):
                paced(low_copy, way, g)
                paced(core_copy, way, g)

    @pl.when(first_col)
    def _():
        for n in range(4):
            @pl.when(first_row | ((y == 1) & (n < 2)))
            def _(n=n):
                corner_copy(n, 1).wait_send()

            @pl.when(first_row | ((y == 3) & (n >= 2)))
            def _(n=n):
                corner_copy(n, -1).wait_send()

    for way in (0, 1):
        @pl.when(jnp.logical_not(first_col | hold_low(way)))
        def _(way=way):
            @pl.when(jnp.logical_not(first_row))
            def _():
                arrivals(low_copy, way, 0, PART)

            arrivals(low_copy, way, PART, total)

        @pl.when((y != 0) & (up_hops[way] == 3) & jnp.logical_not(first_col))
        def _(way=way):
            arrivals(up_copy, way, 0, total)

        @pl.when((up_hops[way] < 3) & jnp.logical_not(first_col))
        def _(way=way):
            drain(up_copy, way)

        @pl.when(first_col | (hold_low(way) & (low_hops[way] < 3)))
        def _(way=way):
            drain(low_copy, way)

        @pl.when(first_col | hold_low(way))
        def _(way=way):
            drain(core_copy, way)


def share(full, inverse, pattern):
    dma = pltpu.SemaphoreType.DMA((2 * 2 * PIECES,))
    return pl.pallas_call(
        share_kernel,
        out_shape=(
            pltpu.VMEM((ROWS, 2 * PANEL), BF16),
            pltpu.VMEM((2 * PANEL, COLS), BF16),
            pltpu.VMEM((ROWS, COLS), F32),
            pltpu.VMEM((PANEL, COLS), F32),
        ),
        in_specs=[VMEM, ANY, SMEM],
        out_specs=(VMEM, VMEM, VMEM, VMEM),
        scratch_shapes=[
            pltpu.VMEM((2, PANEL, PANEL), F32),
            pltpu.VMEM((2, PANEL, PANEL), BF16),
            pltpu.VMEM((2, PANEL, PANEL), BF16),
            dma,
            dma,
            dma,
            dma,
            dma,
            pltpu.SemaphoreType.DMA((8,)),
            pltpu.SemaphoreType.DMA((4,)),
            pltpu.SemaphoreType.DMA,
        ],
        compiler_params=pltpu.CompilerParams(
            collective_id=1, has_side_effects=True, vmem_limit_bytes=SCOPED
        ),
        name="share",
    )(full, inverse, pattern)


BLOCK = 512


def update_kernel(pattern, full, low, up, mat, pivot_rows, out, slots, sems):
    row = lax.axis_index("row")
    col = lax.axis_index("col")
    first_col = col == 0
    first_row = row == 0

    def store(source, block):
        return pltpu.make_async_copy(source, out.at[rows_of(block, BLOCK)], sems.at[lax.rem(block, 2)])

    @pl.when(first_col)
    def _():
        copy = pltpu.make_async_copy(mat, out, sems.at[2])
        copy.start()
        copy.wait()

    @pl.when(jnp.logical_not(first_col))
    def _():
        start = jnp.where(first_row, 2, 0)
        above = [
            pltpu.make_async_copy(full.at[0:PANEL], out.at[0:PANEL], sems.at[2]),
            pltpu.make_async_copy(pivot_rows, out.at[PANEL : 2 * PANEL], sems.at[3]),
        ]

        @pl.when(first_row)
        def _():
            for copy in above:
                copy.start()

        @pl.loop(start, ROWS // BLOCK)
        def _(block):
            rows = rows_of(block, BLOCK)
            slot = lax.rem(block, 2)

            @pl.when(block >= start + 2)
            def _():
                store(slots.at[slot], block).wait()

            cut = jnp.dot(low[rows, :], up[...], preferred_element_type=F32)
            for m in range(BLOCK // TILE):
                here = pl.ds(pl.multiple_of(block * BLOCK + m * TILE, TILE), TILE)
                tile = slice(m * TILE, (m + 1) * TILE)
                for c in range(COLS // TILE):
                    cols = slice(c * TILE, (c + 1) * TILE)
                    keep = pattern[row * 16 + block * (BLOCK // TILE) + m, col * 8 + c].astype(F32)
                    slots[slot, tile, cols] = full[here, cols] - cut[tile, cols] * keep
            store(slots.at[slot], block).start()

        for block in (2, 3):
            store(slots.at[block % 2], block).wait()

        @pl.when(first_row)
        def _():
            for copy in above:
                copy.wait()


def update(pattern, full, low, up, mat, pivot_rows):
    return pl.pallas_call(
        update_kernel,
        out_shape=jax.ShapeDtypeStruct((ROWS, COLS), F32),
        in_specs=[SMEM, VMEM, VMEM, VMEM, VMEM, VMEM],
        out_specs=ANY,
        scratch_shapes=[pltpu.VMEM((2, BLOCK, COLS), F32), pltpu.SemaphoreType.DMA((4,))],
        compiler_params=pltpu.CompilerParams(vmem_limit_bytes=SCOPED),
        name="update",
    )(pattern, full, low, up, mat, pivot_rows)


def body(front_in, child_tiles, child_map, pattern, pivot_inverse):
    kids, maps, front = exchange(child_tiles, child_map, front_in)
    full = assemble(maps, kids.reshape(-1, TILE, TILE), front)
    low, up, mat, pivot_rows = share(full, pivot_inverse, pattern)
    return update(pattern, full, low, up, mat, pivot_rows)


def solution(mesh):
    return jax.shard_map(
        body,
        mesh=mesh,
        in_specs=(
            P(("front", "row"), "col"),
            P(("front", "row", "col"), None, None, None),
            P(("front", "row", "col"), None),
            P("front", None),
            P("front", None, None),
        ),
        out_specs=P(("front", "row"), "col"),
        check_vma=False,
    )
```

```python
import functools

import jax
import jax.numpy as jnp
from jax import lax
from jax.experimental import pallas as pl
from jax.experimental.pallas import tpu as pltpu
from jax.sharding import PartitionSpec as P

TILE = 128
PANEL = 512
SLOTS = 7
NT = 64
ROWS = 2048
COLS = 1024
MESH = pl.DeviceIdType.MESH
ANY = pl.BlockSpec(memory_space=pl.ANY)
VMEM = pl.BlockSpec(memory_space=pltpu.VMEM)
SMEM = pl.BlockSpec(memory_space=pltpu.SMEM)
HBM = pl.BlockSpec(memory_space=pltpu.HBM)
F32 = jnp.float32
BF16 = jnp.bfloat16
SCOPED = 16 << 20


def position():
    col = lax.axis_index("col")
    return lax.axis_index("front"), lax.axis_index("row"), col // 2, lax.rem(col, 2)


def mod4(v):
    return lax.rem(v + 8, 4)


def device(x, y, z, k):
    return (x, mod4(y), mod4(z) * 2 + k)


def remote(src, dst, send, recv, to):
    return pltpu.make_async_remote_copy(src, dst, send, recv, device_id=to, device_id_type=MESH)


def hail(peers):
    for peer in peers:
        pl.semaphore_signal(pltpu.get_barrier_semaphore(), inc=1, device_id=peer, device_id_type=MESH)
    return len(peers)


def greet(peers):
    pl.semaphore_wait(pltpu.get_barrier_semaphore(), hail(peers))


STEPS = (1, 3, 2)
TURNS = ((1, 3), (3, 1), (2, 2), (3, 3), (1, 1), (2, 1), (1, 2), (3, 2), (2, 3))


def exchange_kernel(src, own_map, front, dst, maps, acc, mid, send, recv, map_send, map_recv, local):
    x, y, z, k = position()
    other = 1 - k
    me = y * 8 + z * 2 + k

    def partner(d):
        to = lax.rem(me + d, 32)
        return x, to // 8, lax.rem(to, 8)

    greet([partner(d) for d in range(1, 32)])
    count = 0

    def send_to(block, target, to):
        nonlocal count
        copy = remote(block, target, send.at[count], recv.at[count], to)
        copy.start()
        count += 1
        return copy

    first = []
    for a, b in TURNS:
        first.append(
            (
                send_to(src.at[mod4(y + a), mod4(z + b), k], mid.at[0, a, b], device(x, y + a, z, k)),
                send_to(src.at[mod4(y + b), mod4(z + a), other], mid.at[1, a, b], device(x, y, z + a, other)),
                a,
                b,
            )
        )

    def map_copy(d):
        return remote(own_map, maps.at[me], map_send.at[d], map_recv.at[d], partner(d))

    @pl.loop(1, 32)
    def _(d):
        map_copy(d).start()

    rest = []
    for d in STEPS:
        rest.append(send_to(src.at[mod4(y + d), z, k], dst.at[y, z, k], device(x, y + d, z, k)))
        rest.append(send_to(src.at[y, mod4(z + d), k], dst.at[y, z, k], device(x, y, z + d, k)))
        rest.append(send_to(src.at[mod4(y + d), z, other], dst.at[y, z, k], device(x, y + d, z, other)))
        rest.append(send_to(src.at[y, mod4(z + d), other], dst.at[y, z, k], device(x, y, z + d, other)))
    rest.append(send_to(src.at[y, z, other], dst.at[y, z, k], device(x, y, z, other)))
    own = [
        pltpu.make_async_copy(src.at[y, z, k], dst.at[y, z, k], local.at[0]),
        pltpu.make_async_copy(own_map, maps.at[me], local.at[1]),
        pltpu.make_async_copy(front, acc, local.at[2]),
    ]
    for copy in own:
        copy.start()
    for by_row, by_col, a, b in first:
        by_row.wait_recv()
        rest.append(send_to(mid.at[0, a, b], dst.at[mod4(y - a), z, k], device(x, y, z + b, k)))
        by_col.wait_recv()
        rest.append(send_to(mid.at[1, a, b], dst.at[y, mod4(z - a), other], device(x, y + b, z, k)))
    for by_row, by_col, _, _ in first:
        by_row.wait_send()
        by_col.wait_send()
    for copy in own:
        copy.wait()

    @pl.loop(1, 32)
    def _(d):
        map_copy(d).wait()

    for copy in rest:
        copy.wait()


def exchange(tiles, child_map, front):
    shape = (4, 4, 2, SLOTS, TILE, TILE)
    copies = 18 + 13 + 18
    return pl.pallas_call(
        exchange_kernel,
        out_shape=(
            pltpu.VMEM(shape, tiles.dtype),
            jax.ShapeDtypeStruct((32, *child_map.shape), child_map.dtype),
            pltpu.VMEM(front.shape, front.dtype),
            jax.ShapeDtypeStruct((2, 4, 4, SLOTS, TILE, TILE), tiles.dtype),
        ),
        in_specs=[HBM, HBM, HBM],
        out_specs=(VMEM, ANY, VMEM, HBM),
        scratch_shapes=[
            pltpu.SemaphoreType.DMA((copies,)),
            pltpu.SemaphoreType.DMA((copies,)),
            pltpu.SemaphoreType.DMA((32,)),
            pltpu.SemaphoreType.DMA((32,)),
            pltpu.SemaphoreType.DMA((3,)),
        ],
        compiler_params=pltpu.CompilerParams(
            collective_id=0, has_side_effects=True, vmem_limit_bytes=SCOPED
        ),
        name="exchange",
    )(*(pltpu.with_memory_space_constraint(v, pltpu.HBM) for v in (tiles.reshape(shape), child_map, front)))[:3]


def split(x):
    high = x.astype(BF16)
    return high, (x - high.astype(F32)).astype(BF16)


def wide_dot(a, b_high, b_low):
    a_high, a_low = split(a)
    dot = functools.partial(jnp.dot, preferred_element_type=F32)
    return dot(a_high, b_high) + (dot(a_low, b_high) + dot(a_high, b_low))


def assemble_kernel(maps, kids, front, full):
    row = lax.axis_index("row")
    col = lax.axis_index("col")
    first = (row * 8 + col) * SLOTS

    @pl.loop(0, 32)
    def _(source):
        for slot in range(SLOTS):
            t = maps[source, 0, first + slot]
            r = pl.multiple_of((t // NT - row * 16) * TILE, TILE)
            c = pl.multiple_of((lax.rem(t, NT) - col * 8) * TILE, TILE)
            full[pl.ds(r, TILE), pl.ds(c, TILE)] += kids[source * SLOTS + slot].astype(F32)


def assemble(maps, kids, front):
    return pl.pallas_call(
        assemble_kernel,
        out_shape=pltpu.VMEM((ROWS, COLS), F32),
        in_specs=[SMEM, VMEM, VMEM],
        out_specs=VMEM,
        input_output_aliases={2: 0},
        compiler_params=pltpu.CompilerParams(vmem_limit_bytes=SCOPED),
        name="assemble",
    )(maps, kids, front)


PART = 2
PIECES = 4 * PART
WINDOW = 3
SKEW = 2
LEAD = 2
GAP = max(0, 2 * SKEW + LEAD + PART - 1 - PIECES)

UPDATE_AT = PIECES + 3 * SKEW + LEAD


def rows_of(chunk, count):
    return pl.ds(pl.multiple_of(chunk * count, count), count)


def lower_group(i):
    return lax.rem(i // PART + 1, 4)


def upper_chunk(way, i):
    q = i // PART
    return lax.rem(q // 2 * 4 + 4, 8) + 2 * way + lax.rem(q, 2)


def share_kernel(
    full, inverse, pattern, low, up, mat, pivot_rows,
    inv_high, inv_low, send_low, recv_low, send_core, send_up, recv_up, send_corner, recv_corner, send_again
):
    x, y, z, k = position()
    first_row = y == 0
    first_col = (z == 0) & (k == 0)
    down = device(x, y + 1, z, k), device(x, y - 1, z, k)
    across = device(x, y, z, 1 - k)
    ahead = device(x, y, z + 1, 0), device(x, y, z - 1, 1)
    low_hops = z, mod4(-z)
    up_hops = y, mod4(-y)

    def kept(chunk, tile_col):
        return pattern[y * 16 + chunk, (z * 2 + k) * 8 + tile_col].astype(F32)

    seeds = first_row & jnp.logical_not(first_col)
    def make_low(g):
        group = lower_group(lax.rem(g, PIECES))
        rows = rows_of(group, PANEL)
        solved = (y > 0) | (group >= 1)

        @pl.when(g < PIECES)
        def _():
            part = wide_dot(full[rows, 0:PANEL], inv_high[0], inv_low[0])
            low[rows, 0:PANEL] = part.astype(BF16)
            mat[rows, PANEL:] = full[rows, PANEL:]

            @pl.when(solved)
            def _():
                mat[rows, 0:PANEL] = part

            @pl.when(jnp.logical_not(solved))
            def _():
                mat[rows, 0:PANEL] = full[rows, 0:PANEL]

        @pl.when((g >= PIECES) & solved)
        def _():
            cut = jnp.dot(low[rows, 0:PANEL], up[0:PANEL, PANEL:], preferred_element_type=F32)
            for m in range(4):
                for n in range(4):
                    here = pl.ds(pl.multiple_of(group * PANEL + m * TILE, TILE), TILE)
                    cols = slice(PANEL + n * TILE, PANEL + (n + 1) * TILE)
                    mat[here, cols] -= cut[m * TILE : (m + 1) * TILE, n * TILE : (n + 1) * TILE] * kept(
                        group * 4 + m, 4 + n
                    )
            part = wide_dot(mat[rows, PANEL:], inv_high[1], inv_low[1])
            low[rows, PANEL:] = part.astype(BF16)

            @pl.when((y > 0) | (group >= 2))
            def _():
                mat[rows, PANEL:] = part

        @pl.when((g >= PIECES) & jnp.logical_not(solved))
        def _():
            low[rows, PANEL:] = jnp.zeros((PANEL, PANEL), BF16)

    peers = hail([device(x, y, z + d, c) for d in (1, -1) for c in (k, 1 - k)] + [*down, across])

    def split_inverse(panel):
        high, rest = split(inverse[panel])
        inv_high[panel] = high
        inv_low[panel] = rest

    @pl.when(first_row)
    def _():
        up[0:PANEL, :] = full[0:PANEL, :].astype(BF16)

    @pl.when(first_col)
    def _():
        split_inverse(0)
        make_low(0)

    pl.semaphore_wait(pltpu.get_barrier_semaphore(), peers)

    def low_piece(way, g):
        panel, i = g // PIECES, lax.rem(g, PIECES)
        row = (lower_group(i) * 2 + way) * PART + lax.rem(i, PART)
        return low.at[rows_of(row, 256 // PART), rows_of(panel, PANEL)]

    def low_copy(way, g):
        n = way * 2 * PIECES + g
        piece = low_piece(way, g)
        return remote(piece, piece, send_low.at[n], recv_low.at[n], ahead[way])

    def again(way, g):
        piece = low_piece(way, g)
        to = device(x, y, z - 1 + 2 * way, way)
        return remote(piece, piece, send_again.at[way * PART + g], recv_low.at[way * 2 * PIECES + g], to)

    def core_copy(way, g):
        n = way * 2 * PIECES + g
        piece = low_piece(way, g)
        return remote(piece, piece, send_core.at[n], recv_low.at[n], across)

    def up_copy(way, g):
        n = way * 2 * PIECES + g
        panel, i = g // PIECES, lax.rem(g, PIECES)
        piece = up.at[
            rows_of(panel * PART + lax.rem(i, PART), PANEL // PART), rows_of(upper_chunk(way, i), TILE)
        ]
        return remote(piece, piece, send_up.at[n], recv_up.at[n], down[way])

    def make_up(way, g):
        chunk = upper_chunk(way, lax.rem(g, PIECES))
        cols = rows_of(chunk, TILE)
        cut = jnp.dot(low[PANEL : 2 * PANEL, 0:PANEL], up[0:PANEL, cols], preferred_element_type=F32)
        for n in range(4):
            tile = slice(n * TILE, (n + 1) * TILE)
            value = full[PANEL + n * TILE : PANEL + (n + 1) * TILE, cols] - cut[tile] * kept(4 + n, chunk)
            pivot_rows[tile, cols] = value
            up[PANEL + n * TILE : PANEL + (n + 1) * TILE, cols] = value.astype(BF16)

    def corner_copy(n, d):
        piece = up.at[rows_of(n, TILE), pl.ds(PANEL, PANEL)]
        slot = n if d > 0 else 4 + n
        return remote(piece, piece, send_corner.at[slot], recv_corner.at[n], device(x, y + d, z, k))

    def pass_corner(n):
        for d in (1, -1):
            @pl.when(y == mod4(d))
            def _(d=d):
                copy = corner_copy(n if d > 0 else 2 + n, d)
                copy.wait_recv()
                copy.start()

    @pl.when(first_row & first_col)
    def _():
        for n in range(2):
            for d, piece in ((1, n), (-1, 2 + n)):
                corner_copy(piece, d).start()
        for n in range(2):
            for d, piece in ((1, 2 + n), (-1, n)):
                corner_copy(piece, d).start()

    total = 2 * PIECES

    def due(step):
        second = step >= PIECES + GAP
        return jnp.where(second, step - GAP, step), ((step >= 0) & (step < PIECES)) | (second & (step < total + GAP))

    def paced(copy_of, way, g, unsent=0):
        @pl.when(g >= WINDOW + unsent)
        def _():
            copy_of(way, g - WINDOW).wait_send()

        copy_of(way, g).start()

    def drain(copy_of, way):
        @pl.loop(total - WINDOW, total)
        def _(g):
            copy_of(way, g).wait_send()

    def arrivals(copy_of, way, start, stop):
        @pl.loop(start, stop)
        def _(g):
            copy_of(way, g).wait_recv()

    def hold_low(way):
        return (z != 0) & (k == way)

    def rest_of_first():
        for way in (0, 1):
            @pl.when(jnp.logical_not(hold_low(way)))
            def _(way=way):
                @pl.when(jnp.logical_not(first_row))
                def _():
                    arrivals(low_copy, way, 0, PART)

                arrivals(low_copy, way, PART, PIECES)

            @pl.when((y != 0) & (up_hops[way] == 3))
            def _(way=way):
                arrivals(up_copy, way, 0, PIECES)

    def first_update(block):
        cut = jnp.dot(low[rows_of(block, 256), 0:PANEL], up[0:PANEL, :], preferred_element_type=F32)
        for m in range(2):
            here = rows_of(2 * block + m, TILE)
            for c in range(COLS // TILE):
                cols = slice(c * TILE, (c + 1) * TILE)
                mat[here, cols] = full[here, cols] - cut[m * TILE : (m + 1) * TILE, cols] * kept(2 * block + m, c)

    @pl.loop(0, total + GAP + 3 * SKEW + LEAD)
    def _(t):
        @pl.when(jnp.logical_not(first_col) & (t >= UPDATE_AT))
        def _():
            @pl.when(t == UPDATE_AT)
            def _():
                rest_of_first()

            block = t - UPDATE_AT

            @pl.when((block < ROWS // 256) & ((y > 0) | (block >= 4)))
            def _():
                first_update(block)

        for way in (0, 1):
            j, here = due(t - SKEW * low_hops[way] - LEAD)

            @pl.when(here & hold_low(way))
            def _(way=way, j=j):
                unsent = jnp.where(first_row & (low_hops[way] == 2), PART, 0)

                @pl.when(jnp.logical_not(first_row & (low_hops[way] == 3) & (j < PART)))
                def _():
                    low_copy(way, j).wait_recv()

                    @pl.when((low_hops[way] < 3) & (j >= unsent))
                    def _():
                        paced(low_copy, way, j, unsent)

                    paced(core_copy, way, j)

            early = t - SKEW - LEAD

            @pl.when(first_row & hold_low(way) & (low_hops[way] == 3) & (early >= 0) & (early < PART))
            def _(way=way, early=early):
                low_copy(way, early).wait_recv()
                core_copy(way, early).start()

        for way in (0, 1):
            i, here = due(t - SKEW * up_hops[way] - LEAD)

            @pl.when(here & (y != 0) & (up_hops[way] < 3) & jnp.logical_not(first_col))
            def _(way=way, i=i):
                up_copy(way, i).wait_recv()
                paced(up_copy, way, i)

        g, here = due(t)

        @pl.when(here & seeds)
        def _():
            @pl.when(g == PIECES)
            def _():
                for way in (0, 1):
                    @pl.when(jnp.logical_not(hold_low(way)))
                    def _(way=way):
                        arrivals(low_copy, way, 0, PART)

            for way in (0, 1):
                @pl.when((g >= PIECES) & (lax.rem(g, PART) == 0))
                def _(way=way):
                    make_up(way, g)

                paced(up_copy, way, g)

        @pl.when(here & first_col)
        def _():
            @pl.when(t == 4)
            def _():
                pass_corner(0)

            @pl.when(t == 6)
            def _():
                pass_corner(1)

            @pl.when(g == PIECES)
            def _():
                for n in range(4):
                    @pl.when((y == 2) | ((y == 1) & (n >= 2)) | ((y == 3) & (n < 2)))
                    def _(n=n):
                        corner_copy(n, 1).wait_recv()

            @pl.when(g == PIECES)
            def _():
                split_inverse(1)

            @pl.when((g > 0) & (lax.rem(g, PART) == 0))
            def _():
                make_low(g)

            for way in (0, 1):
                paced(low_copy, way, g)

                @pl.when(first_row & (g < PART))
                def _(way=way):
                    again(way, g).start()

                paced(core_copy, way, g)

    @pl.when(first_row & first_col)
    def _():
        for way in (0, 1):
            for g in range(PART):
                again(way, g).wait_send()

    @pl.when(first_col)
    def _():
        for n in range(4):
            @pl.when(first_row | ((y == 1) & (n < 2)))
            def _(n=n):
                corner_copy(n, 1).wait_send()

            @pl.when(first_row | ((y == 3) & (n >= 2)))
            def _(n=n):
                corner_copy(n, -1).wait_send()

    for way in (0, 1):
        @pl.when(jnp.logical_not(first_col | hold_low(way)))
        def _(way=way):
            arrivals(low_copy, way, PIECES, total)

        @pl.when((y != 0) & (up_hops[way] == 3) & jnp.logical_not(first_col))
        def _(way=way):
            arrivals(up_copy, way, PIECES, total)

        @pl.when((up_hops[way] < 3) & jnp.logical_not(first_col))
        def _(way=way):
            drain(up_copy, way)

        @pl.when(first_col | (hold_low(way) & (low_hops[way] < 3)))
        def _(way=way):
            drain(low_copy, way)

        @pl.when(first_col | hold_low(way))
        def _(way=way):
            drain(core_copy, way)


def share(full, inverse, pattern):
    dma = pltpu.SemaphoreType.DMA((2 * 2 * PIECES,))
    return pl.pallas_call(
        share_kernel,
        out_shape=(
            pltpu.VMEM((ROWS, 2 * PANEL), BF16),
            pltpu.VMEM((2 * PANEL, COLS), BF16),
            pltpu.VMEM((ROWS, COLS), F32),
            pltpu.VMEM((PANEL, COLS), F32),
        ),
        in_specs=[VMEM, VMEM, SMEM],
        out_specs=(VMEM, VMEM, VMEM, VMEM),
        scratch_shapes=[
            pltpu.VMEM((2, PANEL, PANEL), BF16),
            pltpu.VMEM((2, PANEL, PANEL), BF16),
            dma,
            dma,
            dma,
            dma,
            dma,
            pltpu.SemaphoreType.DMA((8,)),
            pltpu.SemaphoreType.DMA((4,)),
            pltpu.SemaphoreType.DMA((2 * PART,)),
        ],
        compiler_params=pltpu.CompilerParams(
            collective_id=1, has_side_effects=True, vmem_limit_bytes=SCOPED
        ),
        name="share",
    )(full, inverse, pattern)


BLOCK = 256
HALF = ROWS // 2


def update_kernel(pattern, full, low, up, mat, pivot_rows, out, slots, sems):
    row = lax.axis_index("row")
    col = lax.axis_index("col")
    first_col = col == 0
    first_row = row == 0

    def store(block, half):
        slot = lax.rem(block, 2)
        rows = pl.ds(half * HALF, HALF)
        return pltpu.make_async_copy(
            slots.at[slot, rows], out.at[rows, rows_of(block, BLOCK)], sems.at[2 * slot + half]
        )

    @pl.when(first_col)
    def _():
        copy = pltpu.make_async_copy(mat, out, sems.at[4])
        copy.start()
        copy.wait()

    @pl.when(jnp.logical_not(first_col))
    def _():
        above = [
            pltpu.make_async_copy(full.at[0:PANEL], out.at[0:PANEL], sems.at[4]),
            pltpu.make_async_copy(pivot_rows, out.at[PANEL : 2 * PANEL], sems.at[5]),
        ]

        @pl.when(first_row)
        def _():
            for copy in above:
                copy.start()

        @pl.loop(0, COLS // BLOCK)
        def _(block):
            slot = lax.rem(block, 2)
            cols = rows_of(block, BLOCK)
            for half in (0, 1):
                @pl.when((row > 0) | (half == 1))
                def _(half=half):
                    @pl.when(block >= 2)
                    def _():
                        store(block, half).wait()

                    cut = jnp.dot(
                        low[half * HALF : (half + 1) * HALF, PANEL:], up[PANEL:, cols], preferred_element_type=F32
                    )
                    for m in range(HALF // TILE):
                        tile = slice(m * TILE, (m + 1) * TILE)
                        here = slice(half * HALF + m * TILE, half * HALF + (m + 1) * TILE)
                        for c in range(BLOCK // TILE):
                            part = slice(c * TILE, (c + 1) * TILE)
                            keep = pattern[
                                row * 16 + half * (HALF // TILE) + m, col * 8 + block * (BLOCK // TILE) + c
                            ].astype(F32)
                            place = rows_of(block * (BLOCK // TILE) + c, TILE)
                            slots[slot, here, part] = mat[here, place] - cut[tile, part] * keep
                    store(block, half).start()

        for block in (2, 3):
            for half in (0, 1):
                @pl.when((row > 0) | (half == 1))
                def _(block=block, half=half):
                    store(block, half).wait()

        @pl.when(first_row)
        def _():
            for copy in above:
                copy.wait()


def update(pattern, full, low, up, mat, pivot_rows):
    return pl.pallas_call(
        update_kernel,
        out_shape=jax.ShapeDtypeStruct((ROWS, COLS), F32),
        in_specs=[SMEM, VMEM, VMEM, VMEM, VMEM, VMEM],
        out_specs=ANY,
        scratch_shapes=[pltpu.VMEM((2, ROWS, BLOCK), F32), pltpu.SemaphoreType.DMA((6,))],
        compiler_params=pltpu.CompilerParams(vmem_limit_bytes=SCOPED),
        name="update",
    )(pattern, full, low, up, mat, pivot_rows)


def body(front_in, child_tiles, child_map, pattern, pivot_inverse):
    kids, maps, front = exchange(child_tiles, child_map, front_in)
    full = assemble(maps, kids.reshape(-1, TILE, TILE), front)
    low, up, mat, pivot_rows = share(full, pivot_inverse, pattern)
    return update(pattern, full, low, up, mat, pivot_rows)


def solution(mesh):
    return jax.shard_map(
        body,
        mesh=mesh,
        in_specs=(
            P(("front", "row"), "col"),
            P(("front", "row", "col"), None, None, None),
            P(("front", "row", "col"), None),
            P("front", None),
            P("front", None, None),
        ),
        out_specs=P(("front", "row"), "col"),
        check_vma=False,
    )
```

```python
import functools

import jax
import jax.numpy as jnp
from jax import lax
from jax.experimental import pallas as pl
from jax.experimental.pallas import tpu as pltpu
from jax.sharding import PartitionSpec as P

TILE = 128
PANEL = 512
SLOTS = 7
NT = 64
ROWS = 2048
COLS = 1024
MESH = pl.DeviceIdType.MESH
ANY = pl.BlockSpec(memory_space=pl.ANY)
VMEM = pl.BlockSpec(memory_space=pltpu.VMEM)
SMEM = pl.BlockSpec(memory_space=pltpu.SMEM)
HBM = pl.BlockSpec(memory_space=pltpu.HBM)
F32 = jnp.float32
BF16 = jnp.bfloat16
SCOPED = 16 << 20


def position():
    col = lax.axis_index("col")
    return lax.axis_index("front"), lax.axis_index("row"), col // 2, lax.rem(col, 2)


def mod4(v):
    return lax.rem(v + 8, 4)


def device(x, y, z, k):
    return (x, mod4(y), mod4(z) * 2 + k)


def remote(src, dst, send, recv, to):
    return pltpu.make_async_remote_copy(src, dst, send, recv, device_id=to, device_id_type=MESH)


def hail(peers):
    for peer in peers:
        pl.semaphore_signal(pltpu.get_barrier_semaphore(), inc=1, device_id=peer, device_id_type=MESH)
    return len(peers)


def greet(peers):
    pl.semaphore_wait(pltpu.get_barrier_semaphore(), hail(peers))


STEPS = (1, 3, 2)
TURNS = ((1, 3), (3, 1), (2, 2), (3, 3), (1, 1), (2, 1), (1, 2), (3, 2), (2, 3))


def exchange_kernel(src, own_map, front, dst, maps, acc, mid, send, recv, map_send, map_recv, local):
    x, y, z, k = position()
    other = 1 - k
    me = y * 8 + z * 2 + k

    def partner(d):
        to = lax.rem(me + d, 32)
        return x, to // 8, lax.rem(to, 8)

    greet([partner(d) for d in range(1, 32)])
    count = 0

    def send_to(block, target, to):
        nonlocal count
        copy = remote(block, target, send.at[count], recv.at[count], to)
        copy.start()
        count += 1
        return copy

    first = []
    for a, b in TURNS:
        first.append(
            (
                send_to(src.at[mod4(y + a), mod4(z + b), k], mid.at[0, a, b], device(x, y + a, z, k)),
                send_to(src.at[mod4(y + b), mod4(z + a), other], mid.at[1, a, b], device(x, y, z + a, other)),
                a,
                b,
            )
        )

    def map_copy(d):
        return remote(own_map, maps.at[me], map_send.at[d], map_recv.at[d], partner(d))

    @pl.loop(1, 32)
    def _(d):
        map_copy(d).start()

    rest = []
    for d in STEPS:
        rest.append(send_to(src.at[mod4(y + d), z, k], dst.at[y, z, k], device(x, y + d, z, k)))
        rest.append(send_to(src.at[y, mod4(z + d), k], dst.at[y, z, k], device(x, y, z + d, k)))
        rest.append(send_to(src.at[mod4(y + d), z, other], dst.at[y, z, k], device(x, y + d, z, other)))
        rest.append(send_to(src.at[y, mod4(z + d), other], dst.at[y, z, k], device(x, y, z + d, other)))
    rest.append(send_to(src.at[y, z, other], dst.at[y, z, k], device(x, y, z, other)))
    own = [
        pltpu.make_async_copy(src.at[y, z, k], dst.at[y, z, k], local.at[0]),
        pltpu.make_async_copy(own_map, maps.at[me], local.at[1]),
        pltpu.make_async_copy(front, acc, local.at[2]),
    ]
    for copy in own:
        copy.start()
    for by_row, by_col, a, b in first:
        by_row.wait_recv()
        rest.append(send_to(mid.at[0, a, b], dst.at[mod4(y - a), z, k], device(x, y, z + b, k)))
        by_col.wait_recv()
        rest.append(send_to(mid.at[1, a, b], dst.at[y, mod4(z - a), other], device(x, y + b, z, k)))
    for by_row, by_col, _, _ in first:
        by_row.wait_send()
        by_col.wait_send()
    for copy in own:
        copy.wait()

    @pl.loop(1, 32)
    def _(d):
        map_copy(d).wait()

    for copy in rest:
        copy.wait()


def exchange(tiles, child_map, front):
    shape = (4, 4, 2, SLOTS, TILE, TILE)
    copies = 18 + 13 + 18
    return pl.pallas_call(
        exchange_kernel,
        out_shape=(
            pltpu.VMEM(shape, tiles.dtype),
            jax.ShapeDtypeStruct((32, *child_map.shape), child_map.dtype),
            pltpu.VMEM(front.shape, front.dtype),
            jax.ShapeDtypeStruct((2, 4, 4, SLOTS, TILE, TILE), tiles.dtype),
        ),
        in_specs=[HBM, HBM, HBM],
        out_specs=(VMEM, ANY, VMEM, HBM),
        scratch_shapes=[
            pltpu.SemaphoreType.DMA((copies,)),
            pltpu.SemaphoreType.DMA((copies,)),
            pltpu.SemaphoreType.DMA((32,)),
            pltpu.SemaphoreType.DMA((32,)),
            pltpu.SemaphoreType.DMA((3,)),
        ],
        compiler_params=pltpu.CompilerParams(
            collective_id=0, has_side_effects=True, vmem_limit_bytes=SCOPED
        ),
        name="exchange",
    )(*(pltpu.with_memory_space_constraint(v, pltpu.HBM) for v in (tiles.reshape(shape), child_map, front)))[:3]


def split(x):
    high = x.astype(BF16)
    return high, (x - high.astype(F32)).astype(BF16)


def wide_dot(a, b_high, b_low):
    a_high, a_low = split(a)
    dot = functools.partial(jnp.dot, preferred_element_type=F32)
    return dot(a_high, b_high) + (dot(a_low, b_high) + dot(a_high, b_low))


def assemble_kernel(maps, kids, front, full):
    row = lax.axis_index("row")
    col = lax.axis_index("col")
    first = (row * 8 + col) * SLOTS

    @pl.loop(0, 32)
    def _(source):
        for slot in range(SLOTS):
            t = maps[source, 0, first + slot]
            r = pl.multiple_of((t // NT - row * 16) * TILE, TILE)
            c = pl.multiple_of((lax.rem(t, NT) - col * 8) * TILE, TILE)
            full[pl.ds(r, TILE), pl.ds(c, TILE)] += kids[source * SLOTS + slot].astype(F32)


def assemble(maps, kids, front):
    return pl.pallas_call(
        assemble_kernel,
        out_shape=pltpu.VMEM((ROWS, COLS), F32),
        in_specs=[SMEM, VMEM, VMEM],
        out_specs=VMEM,
        input_output_aliases={2: 0},
        compiler_params=pltpu.CompilerParams(vmem_limit_bytes=SCOPED),
        name="assemble",
    )(maps, kids, front)


PART = 2
PIECES = 4 * PART
WINDOW = 3
SKEW = 3
LEAD = 1
GAP = max(0, 2 * SKEW + LEAD + PART - 1 - PIECES)

UPDATE_AT = PIECES + 3 * SKEW + LEAD


def rows_of(chunk, count):
    return pl.ds(pl.multiple_of(chunk * count, count), count)


def lower_group(i):
    return lax.rem(i // PART + 1, 4)


def upper_chunk(way, i):
    q = i // PART
    return lax.rem(q // 2 * 4 + 4, 8) + 2 * way + lax.rem(q, 2)


def share_kernel(
    full, inverse, pattern, low, up, mat, pivot_rows,
    inv_high, inv_low, send_low, recv_low, send_core, send_up, recv_up, send_corner, recv_corner, send_again
):
    x, y, z, k = position()
    first_row = y == 0
    first_col = (z == 0) & (k == 0)
    down = device(x, y + 1, z, k), device(x, y - 1, z, k)
    across = device(x, y, z, 1 - k)
    ahead = device(x, y, z + 1, 0), device(x, y, z - 1, 1)
    low_hops = z, mod4(-z)
    up_hops = y, mod4(-y)

    def kept(chunk, tile_col):
        return pattern[y * 16 + chunk, (z * 2 + k) * 8 + tile_col].astype(F32)

    seeds = first_row & jnp.logical_not(first_col)
    def make_low(g):
        group = lower_group(lax.rem(g, PIECES))
        rows = rows_of(group, PANEL)
        solved = (y > 0) | (group >= 1)

        @pl.when(g < PIECES)
        def _():
            part = wide_dot(full[rows, 0:PANEL], inv_high[0], inv_low[0])
            low[rows, 0:PANEL] = part.astype(BF16)
            mat[rows, PANEL:] = full[rows, PANEL:]

            @pl.when(solved)
            def _():
                mat[rows, 0:PANEL] = part

            @pl.when(jnp.logical_not(solved))
            def _():
                mat[rows, 0:PANEL] = full[rows, 0:PANEL]

        @pl.when((g >= PIECES) & solved)
        def _():
            cut = jnp.dot(low[rows, 0:PANEL], up[0:PANEL, PANEL:], preferred_element_type=F32)
            for m in range(4):
                for n in range(4):
                    here = pl.ds(pl.multiple_of(group * PANEL + m * TILE, TILE), TILE)
                    cols = slice(PANEL + n * TILE, PANEL + (n + 1) * TILE)
                    mat[here, cols] -= cut[m * TILE : (m + 1) * TILE, n * TILE : (n + 1) * TILE] * kept(
                        group * 4 + m, 4 + n
                    )
            part = wide_dot(mat[rows, PANEL:], inv_high[1], inv_low[1])
            low[rows, PANEL:] = part.astype(BF16)

            @pl.when((y > 0) | (group >= 2))
            def _():
                mat[rows, PANEL:] = part

        @pl.when((g >= PIECES) & jnp.logical_not(solved))
        def _():
            low[rows, PANEL:] = jnp.zeros((PANEL, PANEL), BF16)

    peers = hail([device(x, y, z + d, c) for d in (1, -1) for c in (k, 1 - k)] + [*down, across])

    def split_inverse(panel):
        high, rest = split(inverse[panel])
        inv_high[panel] = high
        inv_low[panel] = rest

    @pl.when(first_row)
    def _():
        up[0:PANEL, :] = full[0:PANEL, :].astype(BF16)

    @pl.when(first_col)
    def _():
        split_inverse(0)
        make_low(0)

    pl.semaphore_wait(pltpu.get_barrier_semaphore(), peers)

    def low_piece(way, g):
        panel, i = g // PIECES, lax.rem(g, PIECES)
        row = (lower_group(i) * 2 + way) * PART + lax.rem(i, PART)
        return low.at[rows_of(row, 256 // PART), rows_of(panel, PANEL)]

    def low_copy(way, g):
        n = way * 2 * PIECES + g
        piece = low_piece(way, g)
        return remote(piece, piece, send_low.at[n], recv_low.at[n], ahead[way])

    def again(way, g):
        piece = low_piece(way, g)
        to = device(x, y, z - 1 + 2 * way, way)
        return remote(piece, piece, send_again.at[way * PART + g], recv_low.at[way * 2 * PIECES + g], to)

    def core_copy(way, g):
        n = way * 2 * PIECES + g
        piece = low_piece(way, g)
        return remote(piece, piece, send_core.at[n], recv_low.at[n], across)

    def up_copy(way, g):
        n = way * 2 * PIECES + g
        panel, i = g // PIECES, lax.rem(g, PIECES)
        piece = up.at[
            rows_of(panel * PART + lax.rem(i, PART), PANEL // PART), rows_of(upper_chunk(way, i), TILE)
        ]
        return remote(piece, piece, send_up.at[n], recv_up.at[n], down[way])

    def make_up(way, g):
        chunk = upper_chunk(way, lax.rem(g, PIECES))
        cols = rows_of(chunk, TILE)
        cut = jnp.dot(low[PANEL : 2 * PANEL, 0:PANEL], up[0:PANEL, cols], preferred_element_type=F32)
        for n in range(4):
            tile = slice(n * TILE, (n + 1) * TILE)
            value = full[PANEL + n * TILE : PANEL + (n + 1) * TILE, cols] - cut[tile] * kept(4 + n, chunk)
            pivot_rows[tile, cols] = value
            up[PANEL + n * TILE : PANEL + (n + 1) * TILE, cols] = value.astype(BF16)

    def corner_copy(n, d):
        piece = up.at[rows_of(n, TILE), pl.ds(PANEL, PANEL)]
        slot = n if d > 0 else 4 + n
        return remote(piece, piece, send_corner.at[slot], recv_corner.at[n], device(x, y + d, z, k))

    def pass_corner(n):
        for d in (1, -1):
            @pl.when(y == mod4(d))
            def _(d=d):
                copy = corner_copy(n if d > 0 else 2 + n, d)
                copy.wait_recv()
                copy.start()

    @pl.when(first_row & first_col)
    def _():
        for n in range(2):
            for d, piece in ((1, n), (-1, 2 + n)):
                corner_copy(piece, d).start()
        for n in range(2):
            for d, piece in ((1, 2 + n), (-1, n)):
                corner_copy(piece, d).start()

    total = 2 * PIECES

    def due(step):
        second = step >= PIECES + GAP
        return jnp.where(second, step - GAP, step), ((step >= 0) & (step < PIECES)) | (second & (step < total + GAP))

    def paced(copy_of, way, g, unsent=0):
        @pl.when(g >= WINDOW + unsent)
        def _():
            copy_of(way, g - WINDOW).wait_send()

        copy_of(way, g).start()

    def drain(copy_of, way):
        @pl.loop(total - WINDOW, total)
        def _(g):
            copy_of(way, g).wait_send()

    def arrivals(copy_of, way, start, stop):
        @pl.loop(start, stop)
        def _(g):
            copy_of(way, g).wait_recv()

    def hold_low(way):
        return (z != 0) & (k == way)

    def rest_of_first():
        for way in (0, 1):
            @pl.when(jnp.logical_not(hold_low(way)))
            def _(way=way):
                @pl.when(jnp.logical_not(first_row))
                def _():
                    arrivals(low_copy, way, 0, PART)

                arrivals(low_copy, way, PART, PIECES)

            @pl.when((y != 0) & (up_hops[way] == 3))
            def _(way=way):
                arrivals(up_copy, way, 0, PIECES)

    def first_update(block):
        cut = jnp.dot(low[rows_of(block, 256), 0:PANEL], up[0:PANEL, :], preferred_element_type=F32)
        for m in range(2):
            here = rows_of(2 * block + m, TILE)
            for c in range(COLS // TILE):
                cols = slice(c * TILE, (c + 1) * TILE)
                mat[here, cols] = full[here, cols] - cut[m * TILE : (m + 1) * TILE, cols] * kept(2 * block + m, c)

    @pl.loop(0, total + GAP + 3 * SKEW + LEAD)
    def _(t):
        for way in (0, 1):
            j, here = due(t - SKEW * low_hops[way] - LEAD)

            @pl.when(here & hold_low(way))
            def _(way=way, j=j):
                unsent = jnp.where(first_row & (low_hops[way] == 2), PART, 0)

                @pl.when(jnp.logical_not(first_row & (low_hops[way] == 3) & (j < PART)))
                def _():
                    low_copy(way, j).wait_recv()

                    @pl.when((low_hops[way] < 3) & (j >= unsent))
                    def _():
                        paced(low_copy, way, j, unsent)

                    paced(core_copy, way, j)

            early = t - SKEW - LEAD

            @pl.when(first_row & hold_low(way) & (low_hops[way] == 3) & (early >= 0) & (early < PART))
            def _(way=way, early=early):
                low_copy(way, early).wait_recv()
                core_copy(way, early).start()

        for way in (0, 1):
            i, here = due(t - SKEW * up_hops[way] - LEAD)

            @pl.when(here & (y != 0) & (up_hops[way] < 3) & jnp.logical_not(first_col))
            def _(way=way, i=i):
                up_copy(way, i).wait_recv()
                paced(up_copy, way, i)

        g, here = due(t)

        @pl.when(here & seeds)
        def _():
            @pl.when(g == PIECES)
            def _():
                for way in (0, 1):
                    @pl.when(jnp.logical_not(hold_low(way)))
                    def _(way=way):
                        arrivals(low_copy, way, 0, PART)

            for way in (0, 1):
                @pl.when((g >= PIECES) & (lax.rem(g, PART) == 0))
                def _(way=way):
                    make_up(way, g)

                paced(up_copy, way, g)

        @pl.when(here & first_col)
        def _():
            @pl.when(t == 4)
            def _():
                pass_corner(0)

            @pl.when(t == 6)
            def _():
                pass_corner(1)

            @pl.when(g == PIECES)
            def _():
                for n in range(4):
                    @pl.when((y == 2) | ((y == 1) & (n >= 2)) | ((y == 3) & (n < 2)))
                    def _(n=n):
                        corner_copy(n, 1).wait_recv()

            @pl.when(g == PIECES)
            def _():
                split_inverse(1)

            @pl.when((g > 0) & (lax.rem(g, PART) == 0))
            def _():
                make_low(g)

            for way in (0, 1):
                paced(low_copy, way, g)

                @pl.when(first_row & (g < PART))
                def _(way=way):
                    again(way, g).start()

                paced(core_copy, way, g)

        @pl.when(jnp.logical_not(first_col) & (t >= UPDATE_AT))
        def _():
            @pl.when(t == UPDATE_AT)
            def _():
                rest_of_first()

            block = t - UPDATE_AT

            @pl.when((block < ROWS // 256) & ((y > 0) | (block >= 4)))
            def _():
                first_update(block)

    @pl.when(first_row & first_col)
    def _():
        for way in (0, 1):
            for g in range(PART):
                again(way, g).wait_send()

    @pl.when(first_col)
    def _():
        for n in range(4):
            @pl.when(first_row | ((y == 1) & (n < 2)))
            def _(n=n):
                corner_copy(n, 1).wait_send()

            @pl.when(first_row | ((y == 3) & (n >= 2)))
            def _(n=n):
                corner_copy(n, -1).wait_send()

    for way in (0, 1):
        @pl.when(jnp.logical_not(first_col | hold_low(way)))
        def _(way=way):
            arrivals(low_copy, way, PIECES, total)

        @pl.when((y != 0) & (up_hops[way] == 3) & jnp.logical_not(first_col))
        def _(way=way):
            arrivals(up_copy, way, PIECES, total)

        @pl.when((up_hops[way] < 3) & jnp.logical_not(first_col))
        def _(way=way):
            drain(up_copy, way)

        @pl.when(first_col | (hold_low(way) & (low_hops[way] < 3)))
        def _(way=way):
            drain(low_copy, way)

        @pl.when(first_col | hold_low(way))
        def _(way=way):
            drain(core_copy, way)


def share(full, inverse, pattern):
    dma = pltpu.SemaphoreType.DMA((2 * 2 * PIECES,))
    return pl.pallas_call(
        share_kernel,
        out_shape=(
            pltpu.VMEM((ROWS, 2 * PANEL), BF16),
            pltpu.VMEM((2 * PANEL, COLS), BF16),
            pltpu.VMEM((ROWS, COLS), F32),
            pltpu.VMEM((PANEL, COLS), F32),
        ),
        in_specs=[VMEM, VMEM, SMEM],
        out_specs=(VMEM, VMEM, VMEM, VMEM),
        scratch_shapes=[
            pltpu.VMEM((2, PANEL, PANEL), BF16),
            pltpu.VMEM((2, PANEL, PANEL), BF16),
            dma,
            dma,
            dma,
            dma,
            dma,
            pltpu.SemaphoreType.DMA((8,)),
            pltpu.SemaphoreType.DMA((4,)),
            pltpu.SemaphoreType.DMA((2 * PART,)),
        ],
        compiler_params=pltpu.CompilerParams(
            collective_id=1, has_side_effects=True, vmem_limit_bytes=SCOPED
        ),
        name="share",
    )(full, inverse, pattern)


BLOCK = 256
HALF = ROWS // 2


def update_kernel(pattern, full, low, up, mat, pivot_rows, out, slots, sems):
    row = lax.axis_index("row")
    col = lax.axis_index("col")
    first_col = col == 0
    first_row = row == 0

    def store(block, half):
        slot = lax.rem(block, 2)
        rows = pl.ds(half * HALF, HALF)
        return pltpu.make_async_copy(
            slots.at[slot, rows], out.at[rows, rows_of(block, BLOCK)], sems.at[2 * slot + half]
        )

    @pl.when(first_col)
    def _():
        copy = pltpu.make_async_copy(mat, out, sems.at[4])
        copy.start()
        copy.wait()

    @pl.when(jnp.logical_not(first_col))
    def _():
        above = [
            pltpu.make_async_copy(full.at[0:PANEL], out.at[0:PANEL], sems.at[4]),
            pltpu.make_async_copy(pivot_rows, out.at[PANEL : 2 * PANEL], sems.at[5]),
        ]

        @pl.when(first_row)
        def _():
            for copy in above:
                copy.start()

        @pl.loop(0, COLS // BLOCK)
        def _(block):
            slot = lax.rem(block, 2)
            cols = rows_of(block, BLOCK)
            for half in (0, 1):
                @pl.when((row > 0) | (half == 1))
                def _(half=half):
                    @pl.when(block >= 2)
                    def _():
                        store(block, half).wait()

                    cut = jnp.dot(
                        low[half * HALF : (half + 1) * HALF, PANEL:], up[PANEL:, cols], preferred_element_type=F32
                    )
                    for m in range(HALF // TILE):
                        tile = slice(m * TILE, (m + 1) * TILE)
                        here = slice(half * HALF + m * TILE, half * HALF + (m + 1) * TILE)
                        for c in range(BLOCK // TILE):
                            part = slice(c * TILE, (c + 1) * TILE)
                            keep = pattern[
                                row * 16 + half * (HALF // TILE) + m, col * 8 + block * (BLOCK // TILE) + c
                            ].astype(F32)
                            place = rows_of(block * (BLOCK // TILE) + c, TILE)
                            slots[slot, here, part] = mat[here, place] - cut[tile, part] * keep
                    store(block, half).start()

        for block in (2, 3):
            for half in (0, 1):
                @pl.when((row > 0) | (half == 1))
                def _(block=block, half=half):
                    store(block, half).wait()

        @pl.when(first_row)
        def _():
            for copy in above:
                copy.wait()


def update(pattern, full, low, up, mat, pivot_rows):
    return pl.pallas_call(
        update_kernel,
        out_shape=jax.ShapeDtypeStruct((ROWS, COLS), F32),
        in_specs=[SMEM, VMEM, VMEM, VMEM, VMEM, VMEM],
        out_specs=ANY,
        scratch_shapes=[pltpu.VMEM((2, ROWS, BLOCK), F32), pltpu.SemaphoreType.DMA((6,))],
        compiler_params=pltpu.CompilerParams(vmem_limit_bytes=SCOPED),
        name="update",
    )(pattern, full, low, up, mat, pivot_rows)


def body(front_in, child_tiles, child_map, pattern, pivot_inverse):
    kids, maps, front = exchange(child_tiles, child_map, front_in)
    full = assemble(maps, kids.reshape(-1, TILE, TILE), front)
    low, up, mat, pivot_rows = share(full, pivot_inverse, pattern)
    return update(pattern, full, low, up, mat, pivot_rows)


def solution(mesh):
    return jax.shard_map(
        body,
        mesh=mesh,
        in_specs=(
            P(("front", "row"), "col"),
            P(("front", "row", "col"), None, None, None),
            P(("front", "row", "col"), None),
            P("front", None),
            P("front", None, None),
        ),
        out_specs=P(("front", "row"), "col"),
        check_vma=False,
    )
```

```python
import functools

import jax
import jax.numpy as jnp
from jax import lax
from jax.experimental import pallas as pl
from jax.experimental.pallas import tpu as pltpu
from jax.sharding import PartitionSpec as P

TILE = 128
PANEL = 512
SLOTS = 7
NT = 64
ROWS = 2048
COLS = 1024
MESH = pl.DeviceIdType.MESH
ANY = pl.BlockSpec(memory_space=pl.ANY)
VMEM = pl.BlockSpec(memory_space=pltpu.VMEM)
SMEM = pl.BlockSpec(memory_space=pltpu.SMEM)
HBM = pl.BlockSpec(memory_space=pltpu.HBM)
F32 = jnp.float32
BF16 = jnp.bfloat16
SCOPED = 16 << 20


def position():
    col = lax.axis_index("col")
    return lax.axis_index("front"), lax.axis_index("row"), col // 2, lax.rem(col, 2)


def mod4(v):
    return lax.rem(v + 8, 4)


def device(x, y, z, k):
    return (x, mod4(y), mod4(z) * 2 + k)


def remote(src, dst, send, recv, to):
    return pltpu.make_async_remote_copy(src, dst, send, recv, device_id=to, device_id_type=MESH)


def hail(peers):
    for peer in peers:
        pl.semaphore_signal(pltpu.get_barrier_semaphore(), inc=1, device_id=peer, device_id_type=MESH)
    return len(peers)


def greet(peers):
    pl.semaphore_wait(pltpu.get_barrier_semaphore(), hail(peers))


STEPS = (1, 3, 2)
TURNS = ((1, 3), (3, 1), (2, 2), (3, 3), (1, 1), (2, 1), (1, 2), (3, 2), (2, 3))


def exchange_kernel(src, own_map, front, dst, maps, acc, mid, send, recv, map_send, map_recv, local):
    x, y, z, k = position()
    other = 1 - k
    me = y * 8 + z * 2 + k

    def partner(d):
        to = lax.rem(me + d, 32)
        return x, to // 8, lax.rem(to, 8)

    greet([partner(d) for d in range(1, 32)])
    count = 0

    def send_to(block, target, to):
        nonlocal count
        copy = remote(block, target, send.at[count], recv.at[count], to)
        copy.start()
        count += 1
        return copy

    first = []
    for a, b in TURNS:
        first.append(
            (
                send_to(src.at[mod4(y + a), mod4(z + b), k], mid.at[0, a, b], device(x, y + a, z, k)),
                send_to(src.at[mod4(y + b), mod4(z + a), other], mid.at[1, a, b], device(x, y, z + a, other)),
                a,
                b,
            )
        )

    def map_copy(d):
        return remote(own_map, maps.at[me], map_send.at[d], map_recv.at[d], partner(d))

    @pl.loop(1, 32)
    def _(d):
        map_copy(d).start()

    rest = []
    for d in STEPS:
        rest.append(send_to(src.at[mod4(y + d), z, k], dst.at[y, z, k], device(x, y + d, z, k)))
        rest.append(send_to(src.at[y, mod4(z + d), k], dst.at[y, z, k], device(x, y, z + d, k)))
        rest.append(send_to(src.at[mod4(y + d), z, other], dst.at[y, z, k], device(x, y + d, z, other)))
        rest.append(send_to(src.at[y, mod4(z + d), other], dst.at[y, z, k], device(x, y, z + d, other)))
    rest.append(send_to(src.at[y, z, other], dst.at[y, z, k], device(x, y, z, other)))
    own = [
        pltpu.make_async_copy(src.at[y, z, k], dst.at[y, z, k], local.at[0]),
        pltpu.make_async_copy(own_map, maps.at[me], local.at[1]),
        pltpu.make_async_copy(front, acc, local.at[2]),
    ]
    for copy in own:
        copy.start()
    for by_row, by_col, a, b in first:
        by_row.wait_recv()
        rest.append(send_to(mid.at[0, a, b], dst.at[mod4(y - a), z, k], device(x, y, z + b, k)))
        by_col.wait_recv()
        rest.append(send_to(mid.at[1, a, b], dst.at[y, mod4(z - a), other], device(x, y + b, z, k)))
    for by_row, by_col, _, _ in first:
        by_row.wait_send()
        by_col.wait_send()
    for copy in own:
        copy.wait()

    @pl.loop(1, 32)
    def _(d):
        map_copy(d).wait()

    for copy in rest:
        copy.wait()


def exchange(tiles, child_map, front):
    shape = (4, 4, 2, SLOTS, TILE, TILE)
    copies = 18 + 13 + 18
    return pl.pallas_call(
        exchange_kernel,
        out_shape=(
            pltpu.VMEM(shape, tiles.dtype),
            jax.ShapeDtypeStruct((32, *child_map.shape), child_map.dtype),
            pltpu.VMEM(front.shape, front.dtype),
            jax.ShapeDtypeStruct((2, 4, 4, SLOTS, TILE, TILE), tiles.dtype),
        ),
        in_specs=[HBM, HBM, HBM],
        out_specs=(VMEM, ANY, VMEM, HBM),
        scratch_shapes=[
            pltpu.SemaphoreType.DMA((copies,)),
            pltpu.SemaphoreType.DMA((copies,)),
            pltpu.SemaphoreType.DMA((32,)),
            pltpu.SemaphoreType.DMA((32,)),
            pltpu.SemaphoreType.DMA((3,)),
        ],
        compiler_params=pltpu.CompilerParams(
            collective_id=0, has_side_effects=True, vmem_limit_bytes=SCOPED
        ),
        name="exchange",
    )(*(pltpu.with_memory_space_constraint(v, pltpu.HBM) for v in (tiles.reshape(shape), child_map, front)))[:3]


def split(x):
    high = x.astype(BF16)
    return high, (x - high.astype(F32)).astype(BF16)


def wide_dot(a, b_high, b_low):
    a_high, a_low = split(a)
    dot = functools.partial(jnp.dot, preferred_element_type=F32)
    return dot(a_high, b_high) + (dot(a_low, b_high) + dot(a_high, b_low))


def assemble_kernel(maps, kids, front, full):
    row = lax.axis_index("row")
    col = lax.axis_index("col")
    first = (row * 8 + col) * SLOTS

    @pl.loop(0, 32)
    def _(source):
        for slot in range(SLOTS):
            t = maps[source, 0, first + slot]
            r = pl.multiple_of((t // NT - row * 16) * TILE, TILE)
            c = pl.multiple_of((lax.rem(t, NT) - col * 8) * TILE, TILE)
            full[pl.ds(r, TILE), pl.ds(c, TILE)] += kids[source * SLOTS + slot].astype(F32)


def assemble(maps, kids, front):
    return pl.pallas_call(
        assemble_kernel,
        out_shape=pltpu.VMEM((ROWS, COLS), F32),
        in_specs=[SMEM, VMEM, VMEM],
        out_specs=VMEM,
        input_output_aliases={2: 0},
        compiler_params=pltpu.CompilerParams(vmem_limit_bytes=SCOPED),
        name="assemble",
    )(maps, kids, front)


PART = 2
PIECES = 4 * PART
WINDOW = 3
SKEW = 3
LEAD = 1
GAP = max(0, 2 * SKEW + LEAD + PART - 1 - PIECES)

UPDATE_AT = PIECES + 3 * SKEW + LEAD


def rows_of(chunk, count):
    return pl.ds(pl.multiple_of(chunk * count, count), count)


def lower_group(i):
    return lax.rem(i // PART + 1, 4)


def upper_chunk(way, i):
    q = i // PART
    return lax.rem(q // 2 * 4 + 4, 8) + 2 * way + lax.rem(q, 2)


def share_kernel(
    full, inverse, pattern, low, up, mat, pivot_rows,
    inv_high, inv_low, send_low, recv_low, send_core, send_up, recv_up, send_corner, recv_corner, send_again
):
    x, y, z, k = position()
    first_row = y == 0
    first_col = (z == 0) & (k == 0)
    down = device(x, y + 1, z, k), device(x, y - 1, z, k)
    across = device(x, y, z, 1 - k)
    ahead = device(x, y, z + 1, 0), device(x, y, z - 1, 1)
    low_hops = z, mod4(-z)
    up_hops = y, mod4(-y)

    def kept(chunk, tile_col):
        return pattern[y * 16 + chunk, (z * 2 + k) * 8 + tile_col].astype(F32)

    seeds = first_row & jnp.logical_not(first_col)
    def make_low(g):
        group = lower_group(lax.rem(g, PIECES))
        rows = rows_of(group, PANEL)
        solved = (y > 0) | (group >= 1)

        @pl.when(g < PIECES)
        def _():
            part = wide_dot(full[rows, 0:PANEL], inv_high[0], inv_low[0])
            low[rows, 0:PANEL] = part.astype(BF16)
            mat[rows, PANEL:] = full[rows, PANEL:]

            @pl.when(solved)
            def _():
                mat[rows, 0:PANEL] = part

            @pl.when(jnp.logical_not(solved))
            def _():
                mat[rows, 0:PANEL] = full[rows, 0:PANEL]

        @pl.when((g >= PIECES) & solved)
        def _():
            cut = jnp.dot(low[rows, 0:PANEL], up[0:PANEL, PANEL:], preferred_element_type=F32)
            for m in range(4):
                for n in range(4):
                    here = pl.ds(pl.multiple_of(group * PANEL + m * TILE, TILE), TILE)
                    cols = slice(PANEL + n * TILE, PANEL + (n + 1) * TILE)
                    mat[here, cols] -= cut[m * TILE : (m + 1) * TILE, n * TILE : (n + 1) * TILE] * kept(
                        group * 4 + m, 4 + n
                    )
            part = wide_dot(mat[rows, PANEL:], inv_high[1], inv_low[1])
            low[rows, PANEL:] = part.astype(BF16)

            @pl.when((y > 0) | (group >= 2))
            def _():
                mat[rows, PANEL:] = part

        @pl.when((g >= PIECES) & jnp.logical_not(solved))
        def _():
            low[rows, PANEL:] = jnp.zeros((PANEL, PANEL), BF16)

    peers = hail([device(x, y, z + d, c) for d in (1, -1) for c in (k, 1 - k)] + [*down, across])

    def split_inverse(panel):
        high, rest = split(inverse[panel])
        inv_high[panel] = high
        inv_low[panel] = rest

    @pl.when(first_row)
    def _():
        up[0:PANEL, :] = full[0:PANEL, :].astype(BF16)

    @pl.when(first_col)
    def _():
        split_inverse(0)
        make_low(0)

    pl.semaphore_wait(pltpu.get_barrier_semaphore(), peers)

    def low_piece(way, g):
        panel, i = g // PIECES, lax.rem(g, PIECES)
        row = (lower_group(i) * 2 + way) * PART + lax.rem(i, PART)
        return low.at[rows_of(row, 256 // PART), rows_of(panel, PANEL)]

    def low_copy(way, g):
        n = way * 2 * PIECES + g
        piece = low_piece(way, g)
        return remote(piece, piece, send_low.at[n], recv_low.at[n], ahead[way])

    def again(way, g):
        piece = low_piece(way, g)
        to = device(x, y, z - 1 + 2 * way, way)
        return remote(piece, piece, send_again.at[way * PART + g], recv_low.at[way * 2 * PIECES + g], to)

    def core_copy(way, g):
        n = way * 2 * PIECES + g
        piece = low_piece(way, g)
        return remote(piece, piece, send_core.at[n], recv_low.at[n], across)

    def up_copy(way, g):
        n = way * 2 * PIECES + g
        panel, i = g // PIECES, lax.rem(g, PIECES)
        piece = up.at[
            rows_of(panel * PART + lax.rem(i, PART), PANEL // PART), rows_of(upper_chunk(way, i), TILE)
        ]
        return remote(piece, piece, send_up.at[n], recv_up.at[n], down[way])

    def make_up(way, g):
        chunk = upper_chunk(way, lax.rem(g, PIECES))
        cols = rows_of(chunk, TILE)
        cut = jnp.dot(low[PANEL : 2 * PANEL, 0:PANEL], up[0:PANEL, cols], preferred_element_type=F32)
        for n in range(4):
            tile = slice(n * TILE, (n + 1) * TILE)
            value = full[PANEL + n * TILE : PANEL + (n + 1) * TILE, cols] - cut[tile] * kept(4 + n, chunk)
            pivot_rows[tile, cols] = value
            up[PANEL + n * TILE : PANEL + (n + 1) * TILE, cols] = value.astype(BF16)

    def corner_copy(n, d):
        piece = up.at[rows_of(n, TILE), pl.ds(PANEL, PANEL)]
        slot = n if d > 0 else 4 + n
        return remote(piece, piece, send_corner.at[slot], recv_corner.at[n], device(x, y + d, z, k))

    def pass_corner(n):
        for d in (1, -1):
            @pl.when(y == mod4(d))
            def _(d=d):
                copy = corner_copy(n if d > 0 else 2 + n, d)
                copy.wait_recv()
                copy.start()

    @pl.when(first_row & first_col)
    def _():
        for n in range(2):
            for d, piece in ((1, n), (-1, 2 + n)):
                corner_copy(piece, d).start()
        for n in range(2):
            for d, piece in ((1, 2 + n), (-1, n)):
                corner_copy(piece, d).start()

    total = 2 * PIECES

    def due(step):
        second = step >= PIECES + GAP
        return jnp.where(second, step - GAP, step), ((step >= 0) & (step < PIECES)) | (second & (step < total + GAP))

    def paced(copy_of, way, g, unsent=0):
        @pl.when(g >= WINDOW + unsent)
        def _():
            copy_of(way, g - WINDOW).wait_send()

        copy_of(way, g).start()

    def drain(copy_of, way):
        @pl.loop(total - WINDOW, total)
        def _(g):
            copy_of(way, g).wait_send()

    def arrivals(copy_of, way, start, stop):
        @pl.loop(start, stop)
        def _(g):
            copy_of(way, g).wait_recv()

    def hold_low(way):
        return (z != 0) & (k == way)

    def rest_of_first():
        for way in (0, 1):
            @pl.when(jnp.logical_not(hold_low(way)))
            def _(way=way):
                @pl.when(jnp.logical_not(first_row))
                def _():
                    arrivals(low_copy, way, 0, PART)

                arrivals(low_copy, way, PART, PIECES)

            @pl.when((y != 0) & (up_hops[way] == 3))
            def _(way=way):
                arrivals(up_copy, way, 0, PIECES)

    def first_update(block):
        cut = jnp.dot(low[rows_of(block, 256), 0:PANEL], up[0:PANEL, :], preferred_element_type=F32)
        for m in range(2):
            here = rows_of(2 * block + m, TILE)
            for c in range(COLS // TILE):
                cols = slice(c * TILE, (c + 1) * TILE)
                mat[here, cols] = full[here, cols] - cut[m * TILE : (m + 1) * TILE, cols] * kept(2 * block + m, c)

    @pl.loop(0, total + GAP + 3 * SKEW + LEAD)
    def _(t):
        for way in (0, 1):
            j, here = due(t - SKEW * low_hops[way] - LEAD)

            @pl.when(here & hold_low(way))
            def _(way=way, j=j):
                unsent = jnp.where(first_row & (low_hops[way] == 2), PART, 0)

                @pl.when(jnp.logical_not(first_row & (low_hops[way] == 3) & (j < PART)))
                def _():
                    low_copy(way, j).wait_recv()

                    @pl.when((low_hops[way] < 3) & (j >= unsent))
                    def _():
                        paced(low_copy, way, j, unsent)

                    paced(core_copy, way, j)

            early = t - SKEW - LEAD

            @pl.when(first_row & hold_low(way) & (low_hops[way] == 3) & (early >= 0) & (early < PART))
            def _(way=way, early=early):
                low_copy(way, early).wait_recv()
                core_copy(way, early).start()

        for way in (0, 1):
            i, here = due(t - SKEW * up_hops[way] - LEAD)

            @pl.when(here & (y != 0) & (up_hops[way] < 3) & jnp.logical_not(first_col))
            def _(way=way, i=i):
                up_copy(way, i).wait_recv()
                paced(up_copy, way, i)

        g, here = due(t)

        @pl.when(here & seeds)
        def _():
            @pl.when(g == PIECES)
            def _():
                for way in (0, 1):
                    @pl.when(jnp.logical_not(hold_low(way)))
                    def _(way=way):
                        arrivals(low_copy, way, 0, PART)

            for way in (0, 1):
                @pl.when((g >= PIECES) & (lax.rem(g, PART) == 0))
                def _(way=way):
                    make_up(way, g)

                paced(up_copy, way, g)

        @pl.when(here & first_col)
        def _():
            @pl.when(t == 4)
            def _():
                pass_corner(0)

            @pl.when(t == 6)
            def _():
                pass_corner(1)

            @pl.when(g == PIECES)
            def _():
                for n in range(4):
                    @pl.when((y == 2) | ((y == 1) & (n >= 2)) | ((y == 3) & (n < 2)))
                    def _(n=n):
                        corner_copy(n, 1).wait_recv()

            @pl.when(g == PIECES)
            def _():
                split_inverse(1)

            @pl.when((g > 0) & (lax.rem(g, PART) == 0))
            def _():
                make_low(g)

            for way in (0, 1):
                paced(low_copy, way, g)

                @pl.when(first_row & (g < PART))
                def _(way=way):
                    again(way, g).start()

                paced(core_copy, way, g)

        @pl.when(jnp.logical_not(first_col) & (t >= UPDATE_AT))
        def _():
            @pl.when(t == UPDATE_AT)
            def _():
                rest_of_first()

            block = t - UPDATE_AT

            @pl.when((block < ROWS // 256) & ((y > 0) | (block >= 4)))
            def _():
                first_update(block)

    @pl.when(first_row & first_col)
    def _():
        for way in (0, 1):
            for g in range(PART):
                again(way, g).wait_send()

    @pl.when(first_col)
    def _():
        for n in range(4):
            @pl.when(first_row | ((y == 1) & (n < 2)))
            def _(n=n):
                corner_copy(n, 1).wait_send()

            @pl.when(first_row | ((y == 3) & (n >= 2)))
            def _(n=n):
                corner_copy(n, -1).wait_send()

    for way in (0, 1):
        @pl.when(jnp.logical_not(first_col | hold_low(way)))
        def _(way=way):
            arrivals(low_copy, way, PIECES, total)

        @pl.when((y != 0) & (up_hops[way] == 3) & jnp.logical_not(first_col))
        def _(way=way):
            arrivals(up_copy, way, PIECES, total)

        @pl.when((up_hops[way] < 3) & jnp.logical_not(first_col))
        def _(way=way):
            drain(up_copy, way)

        @pl.when(first_col | (hold_low(way) & (low_hops[way] < 3)))
        def _(way=way):
            drain(low_copy, way)

        @pl.when(first_col | hold_low(way))
        def _(way=way):
            drain(core_copy, way)


def share(full, inverse, pattern):
    dma = pltpu.SemaphoreType.DMA((2 * 2 * PIECES,))
    return pl.pallas_call(
        share_kernel,
        out_shape=(
            pltpu.VMEM((ROWS, 2 * PANEL), BF16),
            pltpu.VMEM((2 * PANEL, COLS), BF16),
            pltpu.VMEM((ROWS, COLS), F32),
            pltpu.VMEM((PANEL, COLS), F32),
        ),
        in_specs=[VMEM, VMEM, SMEM],
        out_specs=(VMEM, VMEM, VMEM, VMEM),
        scratch_shapes=[
            pltpu.VMEM((2, PANEL, PANEL), BF16),
            pltpu.VMEM((2, PANEL, PANEL), BF16),
            dma,
            dma,
            dma,
            dma,
            dma,
            pltpu.SemaphoreType.DMA((8,)),
            pltpu.SemaphoreType.DMA((4,)),
            pltpu.SemaphoreType.DMA((2 * PART,)),
        ],
        compiler_params=pltpu.CompilerParams(
            collective_id=1, has_side_effects=True, vmem_limit_bytes=SCOPED
        ),
        name="share",
    )(full, inverse, pattern)


BLOCK = 512
HALF = ROWS // 2


def update_kernel(pattern, full, low, up, mat, pivot_rows, out, slots, sems):
    row = lax.axis_index("row")
    col = lax.axis_index("col")
    first_col = col == 0
    first_row = row == 0

    def store(block, half):
        slot = lax.rem(block, 2)
        rows = pl.ds(half * HALF, HALF)
        return pltpu.make_async_copy(
            slots.at[slot, rows], out.at[rows, rows_of(block, BLOCK)], sems.at[2 * slot + half]
        )

    @pl.when(first_col)
    def _():
        copy = pltpu.make_async_copy(mat, out, sems.at[4])
        copy.start()
        copy.wait()

    @pl.when(jnp.logical_not(first_col))
    def _():
        above = [
            pltpu.make_async_copy(full.at[0:PANEL], out.at[0:PANEL], sems.at[4]),
            pltpu.make_async_copy(pivot_rows, out.at[PANEL : 2 * PANEL], sems.at[5]),
        ]

        @pl.when(first_row)
        def _():
            for copy in above:
                copy.start()

        @pl.loop(0, COLS // BLOCK)
        def _(block):
            slot = lax.rem(block, 2)
            cols = rows_of(block, BLOCK)
            for half in (0, 1):
                @pl.when((row > 0) | (half == 1))
                def _(half=half):
                    @pl.when(block >= 2)
                    def _():
                        store(block, half).wait()

                    cut = jnp.dot(
                        low[half * HALF : (half + 1) * HALF, PANEL:], up[PANEL:, cols], preferred_element_type=F32
                    )
                    for m in range(HALF // TILE):
                        tile = slice(m * TILE, (m + 1) * TILE)
                        here = slice(half * HALF + m * TILE, half * HALF + (m + 1) * TILE)
                        for c in range(BLOCK // TILE):
                            part = slice(c * TILE, (c + 1) * TILE)
                            keep = pattern[
                                row * 16 + half * (HALF // TILE) + m, col * 8 + block * (BLOCK // TILE) + c
                            ].astype(F32)
                            place = rows_of(block * (BLOCK // TILE) + c, TILE)
                            slots[slot, here, part] = mat[here, place] - cut[tile, part] * keep
                    store(block, half).start()

        for block in (0, 1):
            for half in (0, 1):
                @pl.when((row > 0) | (half == 1))
                def _(block=block, half=half):
                    store(block, half).wait()

        @pl.when(first_row)
        def _():
            for copy in above:
                copy.wait()


def update(pattern, full, low, up, mat, pivot_rows):
    return pl.pallas_call(
        update_kernel,
        out_shape=jax.ShapeDtypeStruct((ROWS, COLS), F32),
        in_specs=[SMEM, VMEM, VMEM, VMEM, VMEM, VMEM],
        out_specs=ANY,
        scratch_shapes=[pltpu.VMEM((2, ROWS, BLOCK), F32), pltpu.SemaphoreType.DMA((6,))],
        compiler_params=pltpu.CompilerParams(vmem_limit_bytes=SCOPED),
        name="update",
    )(pattern, full, low, up, mat, pivot_rows)


def body(front_in, child_tiles, child_map, pattern, pivot_inverse):
    kids, maps, front = exchange(child_tiles, child_map, front_in)
    full = assemble(maps, kids.reshape(-1, TILE, TILE), front)
    low, up, mat, pivot_rows = share(full, pivot_inverse, pattern)
    return update(pattern, full, low, up, mat, pivot_rows)


def solution(mesh):
    return jax.shard_map(
        body,
        mesh=mesh,
        in_specs=(
            P(("front", "row"), "col"),
            P(("front", "row", "col"), None, None, None),
            P(("front", "row", "col"), None),
            P("front", None),
            P("front", None, None),
        ),
        out_specs=P(("front", "row"), "col"),
        check_vma=False,
    )
```
